512 devices in a mesh: blk: 128 (over z, x, core), sub: 4 (over y).
Axes of the slice: x: 4, y: 4, z: 16, core: 2. Of those that a mesh axis runs over, the one named last changes fastest.
Arguments:
- features: bfloat16 [16, 1048576], P(None, ('blk', 'sub')), may hold values from -6 to 6
- adjacency: bfloat16 [8192, 8, 128, 128], P(('blk', 'sub')), may hold values from 0.049804688 to 2
- col_tiles: int32 [8192, 8], P(('blk', 'sub')), may hold values from 0 to 8191, as said below
- match_one: int32 [4096, 128], replicated, may hold values from 0 to 127, each once within a row
- match_two: int32 [2048, 128], replicated, may hold values from 0 to 127, each once within a row
Outputs:
- coarse_adjacency: bfloat16 [2048, 8, 128, 128], P(('blk', 'sub'))
- coarse_features: bfloat16 [16, 262144], P(None, ('blk', 'sub'))
The draws below stay inside these ranges and needn't reach their ends.
Inputs may be any that keep to these rules, and one draw needn't show every extreme that they name: `col_tiles`: for each slot k, the two tiles t and t + 64 of a level-one pair ((t // 64) even) name column tiles that differ by 0 or 64; with that difference cleared, the tiles t and t + 16 ((t // 16) even, (t // 64) even) name column tiles that differ by 0 or 16. `match_one`: each row is a matching of the high tile's rows onto the low tile's rows. `match_two`: each row is a matching of the high tile's rows onto the low tile's rows.
All inputs are finite; a program needn't handle non-finite values.
Results may differ from the reference program's by a relative error of at most 0.0053.
Values may be sent and summed in bfloat16 or wider, within the bound.
A program may use at most 64 MiB of HBM per device.

```python
import math
import jax
import jax.numpy as jnp
from jax import lax

FEAT = 16
TILE = 128
NBR = 8
TPD = 16
SPAN = 64
NT = 8192
ROWS = 1048576
PAIRS = 4096
GROUPS = 2048


def draw_col_tiles(key, part):
    key_group, key_sub, key_blk = jax.random.split(key, 3)
    tile_ids = jnp.arange(NT, dtype=jnp.int32)
    pair_ids = tile_ids // (2 * SPAN) * SPAN + tile_ids % SPAN
    group_ids = pair_ids // (2 * TPD) * TPD + pair_ids % TPD
    targets = jax.random.randint(key_group, (GROUPS, NBR), 0, GROUPS, dtype=jnp.int32)
    targets = targets.at[0, 0].set(GROUPS - 1).at[0, 1].set(0)
    sub_bits = jax.random.randint(key_sub, (PAIRS, NBR), 0, 2, dtype=jnp.int32)
    sub_bits = sub_bits.at[0, 0].set(1).at[0, 1].set(0)
    blk_bits = jax.random.randint(key_blk, (NT, NBR), 0, 2, dtype=jnp.int32)
    blk_bits = blk_bits.at[0, 0].set(1).at[0, 1].set(0)
    target_pairs = targets // TPD * 2 * TPD + targets % TPD
    base_tiles = target_pairs // SPAN * 2 * SPAN + target_pairs % SPAN
    return base_tiles[group_ids] + sub_bits[pair_ids] * TPD + blk_bits * SPAN


def shard_levels(key, extent, shards, low, top_value):
    gain, own = 1.0, jax.random.fold_in(key, 6)
    for position, shards_of in shards:
        steps = jnp.exp(jax.random.uniform(jax.random.fold_in(own, position), (shards_of,), jnp.float32, low / len(shards), top_value / len(shards)))
        gain = gain * jnp.repeat(steps, extent[position] // shards_of).reshape([-1 if axis == position else 1 for axis in range(len(extent))])
    return gain


def bell_draw(stream_key, shape, width, bound, cuts=(), held_as=jnp.bfloat16):
    drawn = width * jax.random.normal(stream_key, shape, jnp.float32)
    if cuts:
        drawn = drawn * shard_levels(stream_key, shape, cuts, -0.22, 0.18)
    return jnp.clip(drawn, -bound, bound).astype(held_as)


def setup_inputs(seed: int = 0) -> dict:
    splits = jax.random.split(jax.random.key(seed), 6)
    return {
        "features": bell_draw(splits[0], (FEAT, ROWS), 1.0, 6.0, ((1, 512),)),
        "adjacency": jnp.clip(jnp.exp(math.log(2.0) - 3.6927934 * jax.random.uniform(splits[1], (NT, NBR, TILE, TILE), jnp.float32) ** shard_levels(splits[1], (NT, NBR, TILE, TILE), ((0, 512),), -0.2, 0.2)), 0.049804688, 2.0).astype(jnp.bfloat16),
        "col_tiles": draw_col_tiles(jax.random.fold_in(splits[5], 71), 0),
        "match_one": jax.vmap(lambda own: jax.random.permutation(own, TILE))(jax.random.split(splits[3], PAIRS)).reshape((PAIRS, TILE)).astype(jnp.int32),
        "match_two": jax.vmap(lambda own: jax.random.permutation(own, TILE))(jax.random.split(splits[4], GROUPS)).reshape((GROUPS, TILE)).astype(jnp.int32),
    }


def one_hot(row_maps):
    return (row_maps[..., :, None] == jnp.arange(TILE, dtype=jnp.int32)).astype(jnp.bfloat16)


def pair_of(column_ids):
    return (column_ids // (2 * SPAN)) * SPAN + column_ids % SPAN


def reference(features, adjacency, col_tiles, match_one, match_two):
    positions = jnp.arange(TILE, dtype=jnp.int32)

    def first_map(column_ids):
        upper = (column_ids // SPAN) % 2 == 1
        return jnp.where(upper[..., None], match_one[pair_of(column_ids)], positions)

    def second_map(column_ids):
        pair_index = pair_of(column_ids)
        group_index = (pair_index // (2 * TPD)) * TPD + pair_index % TPD
        upper = (column_ids // TPD) % 2 == 1
        return jnp.where(upper[..., None], match_two[group_index], positions)

    def column_side(blocks, column_ids, mapper):
        return jnp.einsum('kab,kbc->kac', blocks.astype(jnp.float32),
                          one_hot(mapper(column_ids)).astype(jnp.float32))

    feats = features.reshape(FEAT, NT, TILE)

    def level_one(pair_index):
        low_tile = (pair_index // SPAN) * 2 * SPAN + pair_index % SPAN
        high_tile = low_tile + SPAN
        rows_hot = one_hot(match_one[pair_index]).astype(jnp.float32)
        low_term = column_side(adjacency[low_tile], col_tiles[low_tile], first_map)
        high_cols = column_side(adjacency[high_tile], col_tiles[high_tile], first_map)
        high_term = jnp.einsum('ba,kbc->kac', rows_hot, high_cols)
        blocks = (low_term + high_term).astype(jnp.bfloat16)
        low_feat = feats[:, low_tile].astype(jnp.float32)
        high_feat = jnp.dot(feats[:, high_tile].astype(jnp.float32), rows_hot, precision=lax.Precision.HIGHEST)
        merged = (low_feat + high_feat).astype(jnp.bfloat16)
        low_cols = col_tiles[low_tile]
        coarse_cols = low_cols - ((low_cols // SPAN) % 2) * SPAN
        return blocks, merged, coarse_cols

    tiles_one, feats_one, cols_one = lax.map(level_one, jnp.arange(PAIRS, dtype=jnp.int32))

    def level_two(out_index):
        device_index = out_index // (TPD // 4)
        piece_index = out_index % (TPD // 4)
        sub_bit = device_index % 2
        blk_bit = (device_index * TPD // SPAN) % 2
        low_tile = device_index * TPD - sub_bit * TPD - blk_bit * SPAN + 4 * piece_index + 2 * blk_bit + sub_bit
        pair_low = pair_of(low_tile)
        pair_high = pair_low + TPD
        group_index = (pair_low // (2 * TPD)) * TPD + pair_low % TPD
        rows_hot = one_hot(match_two[group_index]).astype(jnp.float32)
        low_term = column_side(tiles_one[pair_low], cols_one[pair_low], second_map)
        high_cols = column_side(tiles_one[pair_high], cols_one[pair_high], second_map)
        high_term = jnp.einsum('ba,kbc->kac', rows_hot, high_cols)
        blocks = (low_term + high_term).astype(jnp.bfloat16)
        high_feat = jnp.dot(feats_one[pair_high].astype(jnp.float32), rows_hot, precision=lax.Precision.HIGHEST)
        merged = (feats_one[pair_low].astype(jnp.float32) + high_feat).astype(jnp.bfloat16)
        return blocks, merged

    tiles_two, feats_two = lax.map(level_two, jnp.arange(GROUPS, dtype=jnp.int32))
    coarse_features = jnp.transpose(feats_two, (1, 0, 2)).reshape(FEAT, GROUPS * TILE)
    return tiles_two, coarse_features
```

```python
import functools

import jax
import jax.numpy as jnp
from jax import lax
from jax.experimental import pallas as pl
from jax.experimental.pallas import tpu as pltpu
from jax.sharding import PartitionSpec as P

MESH = pl.DeviceIdType.MESH
GROUP = 2


def turned(row_map, width):
    down = lax.broadcasted_iota(jnp.int32, (width, width), 0)
    return jnp.where(down == row_map, 1.0, 0.0).astype(jnp.bfloat16)


def right_side(blocks, turned_hot):
    return lax.dot_general(
        blocks, turned_hot, (((1,), (1,)), ((), ())), preferred_element_type=jnp.float32
    )


def merged(low, high, turned_rows, turned_cols):
    width = turned_rows.shape[0]
    moved = jnp.dot(
        turned_rows, jnp.concatenate(high, axis=1), preferred_element_type=jnp.float32
    ).astype(jnp.bfloat16)
    out = []
    for n, block in enumerate(low):
        both = jnp.concatenate([block, moved[:, n * width : (n + 1) * width]], axis=1)
        out.append(right_side(both, turned_cols[n]).astype(jnp.bfloat16))
    return out


def kernel(
    span, feat, adj, cols, m1, m2, out_a, out_f,
    m1v, m2v, col_s, col_1, col_2, adj_v, feat_v, send_a, send_f, lev_a, lev_f, fin_a, fin_f,
    loc_sem, own_sem, put_sem, cs_sem, cr_sem, ss_sem, sr_sem, xs_sem, xr_sem,
):
    tiles, slots, width = adj.shape[0], adj.shape[1], adj.shape[2]
    quarter = tiles // 4
    groups = slots // GROUP
    blk, sub = lax.axis_index("blk"), lax.axis_index("sub")
    b, s = lax.rem(blk, 2), lax.rem(sub, 2)
    core = {"blk": blk + 1 - 2 * b}
    near = {"sub": sub + 1 - 2 * s}
    subs = span // tiles
    first_pair = (blk // 2 * subs + sub) * tiles
    first_group = (blk // 2 * (subs // 2) + sub // 2) * tiles
    lanes = lax.broadcasted_iota(jnp.int32, (1, width), 1)

    def side(j):
        return (1 - s) * (1 - j) + s * j

    def own_copy(j, i, q):
        part = pl.ds(q * GROUP, GROUP)
        return pltpu.make_async_copy(
            adj.at[4 * i + 2 * b + side(j), part], adj_v.at[b, j, i, part], own_sem.at[j, i, q]
        )

    def core_copy(j, i, q):
        part = pl.ds(q * GROUP, GROUP)
        return pltpu.make_async_remote_copy(
            src_ref=adj.at[4 * i + 2 * (1 - b) + side(j), part],
            dst_ref=adj_v.at[b, j, i, part],
            send_sem=cs_sem.at[j, i, q], recv_sem=cr_sem.at[j, i, q],
            device_id=core, device_id_type=MESH,
        )

    def sub_copy(i, q):
        part = pl.ds(q * GROUP, GROUP)
        return pltpu.make_async_remote_copy(
            src_ref=send_a.at[i, part], dst_ref=lev_a.at[s, i, part],
            send_sem=ss_sem.at[i, q], recv_sem=sr_sem.at[i, q],
            device_id=near, device_id_type=MESH,
        )

    def small(src, dst, n, device):
        return pltpu.make_async_remote_copy(
            src_ref=src, dst_ref=dst, send_sem=xs_sem.at[n], recv_sem=xr_sem.at[n],
            device_id=device, device_id_type=MESH,
        )

    def put_copy(i, q):
        part = pl.ds(q * GROUP, GROUP)
        return pltpu.make_async_copy(fin_a.at[i, part], out_a.at[i, part], put_sem.at[i, q])

    barrier = pltpu.get_barrier_semaphore()
    pl.semaphore_signal(barrier, inc=1, device_id=core, device_id_type=MESH)
    pl.semaphore_signal(barrier, inc=1, device_id=near, device_id_type=MESH)

    local = [
        pltpu.make_async_copy(cols, col_s, loc_sem.at[0]),
        pltpu.make_async_copy(cols, col_1.at[b], loc_sem.at[1]),
        pltpu.make_async_copy(cols, col_2.at[s], loc_sem.at[2]),
        pltpu.make_async_copy(m1, m1v, loc_sem.at[3]),
        pltpu.make_async_copy(feat, feat_v.at[b], loc_sem.at[4]),
        pltpu.make_async_copy(m2, m2v, loc_sem.at[5]),
    ]
    for n in range(4):
        local[n].start()
    for q in range(groups):
        own_copy(0, 0, q).start()

    pl.semaphore_wait(barrier, 2)
    cols_core = small(cols, col_1.at[b], 0, core)
    cols_near = small(cols, col_2.at[s], 1, near)
    feat_core = small(feat, feat_v.at[b], 2, core)
    cols_core.start()
    for q in range(groups):
        core_copy(0, 0, q).start()
    cols_near.start()
    feat_core.start()
    local[4].start()

    @pl.loop(1, quarter)
    def _(i):
        for q in range(groups):
            core_copy(0, i, q).start()
            own_copy(0, i, q).start()

    @pl.loop(0, quarter)
    def _(i):
        for q in range(groups):
            core_copy(1, i, q).start()
            own_copy(1, i, q).start()

    local[5].start()

    for n in range(4):
        local[n].wait()
    cols_core.wait()

    def columns(table, maps, tile, k, bit, row):
        here = maps[pl.ds(row, 1), :]
        hots = []
        for part in range(2):
            flags = table[part, pl.ds(tile, 1), :][:, k : k + 1]
            hots.append(turned(jnp.where((flags & bit) != 0, here, lanes), width))
        return jnp.concatenate(hots, axis=1)

    def first_level(j, i, store):
        tile = 4 * i + 2 * b + side(j)
        rows = turned(m1v[pl.ds(first_pair + tile, 1), :], width)
        for q in range(groups):
            own_copy(j, i, q).wait()
            core_copy(j, i, q).wait_recv()
            ks = range(q * GROUP, (q + 1) * GROUP)
            hots = []
            for k in ks:
                c = col_s[tile, k]
                hots.append(
                    columns(col_1, m1v, tile, k, span, c // (2 * span) * span + lax.rem(c, span))
                )
            done = merged(
                [adj_v[0, j, i, k] for k in ks], [adj_v[1, j, i, k] for k in ks], rows, hots
            )
            store(i, q, ks, done)
        return tile, rows

    def feature_level(j, i, tile, rows, dst):
        at = pl.ds(pl.multiple_of(tile * width, width), width)
        total = feat_v[0, :, at].astype(jnp.float32) + right_side(feat_v[1, :, at], rows)
        dst[:, pl.ds(pl.multiple_of(i * width, width), width)] = total.astype(jnp.bfloat16)

    def store_send(i, q, ks, done):
        for k, block in zip(ks, done):
            send_a[i, k] = block
        sub_copy(i, q).start()

    def store_keep(i, q, ks, done):
        for k, block in zip(ks, done):
            lev_a[s, i, k] = block

    @pl.loop(0, quarter)
    def _(i):
        first_level(0, i, store_send)

    local[4].wait()
    feat_core.wait()

    @pl.loop(0, quarter)
    def _(i):
        tile = 4 * i + 2 * b + side(0)
        rows = turned(m1v[pl.ds(first_pair + tile, 1), :], width)
        feature_level(0, i, tile, rows, send_f)

    feat_near = small(send_f, lev_f.at[s], 3, near)
    feat_near.start()

    @pl.loop(0, quarter)
    def _(i):
        tile, rows = first_level(1, i, store_keep)
        feature_level(1, i, tile, rows, lev_f.at[s])

    local[5].wait()
    cols_near.wait()

    @pl.loop(0, quarter)
    def _(i):
        tile = 4 * i + 2 * b + s
        rows = turned(m2v[pl.ds(first_group + tile, 1), :], width)
        for q in range(groups):
            sub_copy(i, q).wait_recv()
            ks = range(q * GROUP, (q + 1) * GROUP)
            hots = []
            for k in ks:
                c = col_s[tile, k]
                p = c // (2 * span) * span + lax.rem(c, span)
                hots.append(
                    columns(col_2, m2v, tile, k, tiles, p // (2 * tiles) * tiles + lax.rem(p, tiles))
                )
            done = merged([lev_a[0, i, k] for k in ks], [lev_a[1, i, k] for k in ks], rows, hots)
            for k, block in zip(ks, done):
                fin_a[i, k] = block
            put_copy(i, q).start()

    feat_near.wait()
    for i in range(quarter):
        tile = 4 * i + 2 * b + s
        rows = turned(m2v[pl.ds(first_group + tile, 1), :], width)
        at = pl.ds(i * width, width)
        total = lev_f[0, :, at].astype(jnp.float32) + right_side(lev_f[1, :, at], rows)
        fin_f[:, at] = total.astype(jnp.bfloat16)
    put_f = pltpu.make_async_copy(fin_f, out_f, loc_sem.at[6])
    put_f.start()

    @pl.loop(0, quarter)
    def _(i):
        for q in range(groups):
            core_copy(0, i, q).wait_send()
            core_copy(1, i, q).wait_send()
            sub_copy(i, q).wait_send()
            put_copy(i, q).wait()

    put_f.wait()


def per_device(features, adjacency, col_tiles, match_one, match_two):
    tiles, slots, width = adjacency.shape[:3]
    feats = features.shape[0]
    quarter, groups = tiles // 4, slots // GROUP
    span = lax.axis_size("sub") * tiles
    half = jnp.bfloat16
    dma = pltpu.SemaphoreType.DMA
    anywhere = pl.BlockSpec(memory_space=pl.ANY)
    return pl.pallas_call(
        functools.partial(kernel, span),
        out_shape=(
            jax.ShapeDtypeStruct((quarter, slots, width, width), half),
            jax.ShapeDtypeStruct((feats, quarter * width), half),
        ),
        in_specs=[anywhere] * 5,
        out_specs=(anywhere, anywhere),
        scratch_shapes=[
            pltpu.VMEM(match_one.shape, jnp.int32),
            pltpu.VMEM(match_two.shape, jnp.int32),
            pltpu.SMEM(col_tiles.shape, jnp.int32),
            pltpu.VMEM((2,) + col_tiles.shape, jnp.int32),
            pltpu.VMEM((2,) + col_tiles.shape, jnp.int32),
            pltpu.VMEM((2, 2, quarter, slots, width, width), half),
            pltpu.VMEM((2,) + features.shape, half),
            pltpu.VMEM((quarter, slots, width, width), half),
            pltpu.VMEM((feats, quarter * width), half),
            pltpu.VMEM((2, quarter, slots, width, width), half),
            pltpu.VMEM((2, feats, quarter * width), half),
            pltpu.VMEM((quarter, slots, width, width), half),
            pltpu.VMEM((feats, quarter * width), half),
            dma((7,)),
            dma((2, quarter, groups)),
            dma((quarter, groups)),
            dma((2, quarter, groups)),
            dma((2, quarter, groups)),
            dma((quarter, groups)),
            dma((quarter, groups)),
            dma((4,)),
            dma((4,)),
        ],
        compiler_params=pltpu.CompilerParams(collective_id=0, has_side_effects=True),
        name="coarsen",
    )(features, adjacency, col_tiles, match_one, match_two)


def solution(mesh):
    placed = (
        P(None, ("blk", "sub")),
        P(("blk", "sub"), None, None, None),
        P(("blk", "sub"), None),
        P(),
        P(),
    )
    return jax.shard_map(
        per_device,
        mesh=mesh,
        in_specs=placed,
        out_specs=(P(("blk", "sub"), None, None, None), P(None, ("blk", "sub"))),
        check_vma=False,
    )
```

```python
import functools

import jax
import jax.numpy as jnp
from jax import lax
from jax.experimental import pallas as pl
from jax.experimental.pallas import tpu as pltpu
from jax.sharding import PartitionSpec as P

MESH = pl.DeviceIdType.MESH
GROUP = 2
VMEM_BYTES = 24 * 2**20


def turned(row_map, width):
    down = lax.broadcasted_iota(jnp.int32, (width, width), 0)
    return jnp.where(down == row_map, 1.0, 0.0).astype(jnp.bfloat16)


def right_side(blocks, turned_hot):
    return lax.dot_general(
        blocks, turned_hot, (((1,), (1,)), ((), ())), preferred_element_type=jnp.float32
    )


def merged(low, high, turned_rows, turned_cols):
    width = turned_rows.shape[0]
    moved = jnp.dot(
        turned_rows, jnp.concatenate(high, axis=1), preferred_element_type=jnp.float32
    ).astype(jnp.bfloat16)
    out = []
    for n, block in enumerate(low):
        both = jnp.concatenate([block, moved[:, n * width : (n + 1) * width]], axis=1)
        out.append(right_side(both, turned_cols[n]).astype(jnp.bfloat16))
    return out


def kernel(
    span, feat, adj, cols, m1, m2, fin_a, fin_f,
    m1v, m2v, col_1, col_2, adj_v, feat_v, send_a, send_f, lev_a, lev_f,
    loc_sem, own_sem, cs_sem, cr_sem, ss_sem, sr_sem, xs_sem, xr_sem,
):
    tiles, slots, width = adj.shape[0], adj.shape[1], adj.shape[2]
    quarter = tiles // 4
    groups = slots // GROUP
    blk, sub = lax.axis_index("blk"), lax.axis_index("sub")
    b, s = lax.rem(blk, 2), lax.rem(sub, 2)
    core = {"blk": blk + 1 - 2 * b}
    near = {"sub": sub + 1 - 2 * s}
    subs = span // tiles
    first_pair = (blk // 2 * subs + sub) * tiles
    first_group = (blk // 2 * (subs // 2) + sub // 2) * tiles
    pairs, pairs2 = m1.shape[0], m2.shape[0]

    def side(j):
        return (1 - s) * (1 - j) + s * j

    def own_copy(j, i, q):
        part = pl.ds(q * GROUP, GROUP)
        return pltpu.make_async_copy(
            adj.at[4 * i + 2 * b + side(j), part], adj_v.at[b, j, i, part], own_sem.at[j, i, q]
        )

    def core_copy(j, i, q):
        part = pl.ds(q * GROUP, GROUP)
        return pltpu.make_async_remote_copy(
            src_ref=adj.at[4 * i + 2 * (1 - b) + side(j), part],
            dst_ref=adj_v.at[b, j, i, part],
            send_sem=cs_sem.at[j, i, q], recv_sem=cr_sem.at[j, i, q],
            device_id=core, device_id_type=MESH,
        )

    def sub_copy(i, k):
        return pltpu.make_async_remote_copy(
            src_ref=send_a.at[i, k], dst_ref=lev_a.at[s, i, k],
            send_sem=ss_sem.at[i, k], recv_sem=sr_sem.at[i, k],
            device_id=near, device_id_type=MESH,
        )

    def small(src, dst, n, device):
        return pltpu.make_async_remote_copy(
            src_ref=src, dst_ref=dst, send_sem=xs_sem.at[n], recv_sem=xr_sem.at[n],
            device_id=device, device_id_type=MESH,
        )

    barrier = pltpu.get_barrier_semaphore()
    pl.semaphore_signal(barrier, inc=1, device_id=core, device_id_type=MESH)
    pl.semaphore_signal(barrier, inc=1, device_id=near, device_id_type=MESH)

    local = [
        pltpu.make_async_copy(m1, m1v.at[pl.ds(0, pairs)], loc_sem.at[0]),
        pltpu.make_async_copy(cols, col_1.at[b], loc_sem.at[1]),
        pltpu.make_async_copy(cols, col_2.at[s], loc_sem.at[2]),
        pltpu.make_async_copy(feat, feat_v.at[b], loc_sem.at[3]),
        pltpu.make_async_copy(m2, m2v.at[pl.ds(0, pairs2)], loc_sem.at[4]),
    ]
    for n in range(3):
        local[n].start()
    for q in range(groups):
        own_copy(0, 0, q).start()

    plain = lax.broadcasted_iota(jnp.int32, (8, width), 1)
    m1v[pl.ds(pairs, 8), :] = plain
    m2v[pl.ds(pairs2, 8), :] = plain

    pl.semaphore_wait(barrier, 2)
    cols_core = small(cols, col_1.at[b], 0, core)
    cols_near = small(cols, col_2.at[s], 1, near)
    feat_core = small(feat, feat_v.at[b], 2, core)
    cols_core.start()
    for q in range(groups):
        core_copy(0, 0, q).start()
    cols_near.start()
    feat_core.start()
    local[3].start()

    @pl.loop(1, quarter)
    def _(i):
        for q in range(groups):
            core_copy(0, i, q).start()
            own_copy(0, i, q).start()

    @pl.loop(0, quarter)
    def _(i):
        for q in range(groups):
            core_copy(1, i, q).start()
            own_copy(1, i, q).start()

    local[4].start()

    for n in range(3):
        local[n].wait()
    cols_core.wait()

    def columns(table, maps, plain_row, tile, k, bit, row):
        hots = []
        for part in range(2):
            upper = lax.rem(table[part, k, tile] // bit, 2)
            here = maps[pl.ds(upper * row + (1 - upper) * plain_row, 1), :]
            hots.append(turned(here, width))
        return jnp.concatenate(hots, axis=1)

    def first_level(j, i, store):
        tile = 4 * i + 2 * b + side(j)
        rows = turned(m1v[pl.ds(first_pair + tile, 1), :], width)
        for q in range(groups):
            own_copy(j, i, q).wait()
            core_copy(j, i, q).wait_recv()
            ks = range(q * GROUP, (q + 1) * GROUP)
            hots = []
            for k in ks:
                c = col_1[0, k, tile]
                p = c // (2 * span) * span + lax.rem(c, span)
                hots.append(columns(col_1, m1v, pairs, tile, k, span, p))
            done = merged(
                [adj_v[0, j, i, k] for k in ks], [adj_v[1, j, i, k] for k in ks], rows, hots
            )
            store(i, q, ks, done)
        return tile, rows

    def feature_level(j, i, tile, rows, dst):
        at = pl.ds(pl.multiple_of(tile * width, width), width)
        total = feat_v[0, :, at].astype(jnp.float32) + right_side(feat_v[1, :, at], rows)
        dst[:, pl.ds(pl.multiple_of(i * width, width), width)] = total.astype(jnp.bfloat16)

    def store_send(i, q, ks, done):
        for k, block in zip(ks, done):
            send_a[i, k] = block
            sub_copy(i, k).start()

    def store_keep(i, q, ks, done):
        for k, block in zip(ks, done):
            lev_a[s, i, k] = block

    @pl.loop(0, quarter)
    def _(i):
        first_level(0, i, store_send)

    local[3].wait()
    feat_core.wait()

    @pl.loop(0, quarter)
    def _(i):
        tile = 4 * i + 2 * b + side(0)
        rows = turned(m1v[pl.ds(first_pair + tile, 1), :], width)
        feature_level(0, i, tile, rows, send_f)

    feat_near = small(send_f, lev_f.at[s], 3, near)
    feat_near.start()

    @pl.loop(0, quarter)
    def _(i):
        tile, rows = first_level(1, i, store_keep)
        feature_level(1, i, tile, rows, lev_f.at[s])

    local[4].wait()
    cols_near.wait()

    @pl.loop(0, quarter)
    def _(i):
        tile = 4 * i + 2 * b + s
        rows = turned(m2v[pl.ds(first_group + tile, 1), :], width)
        for k in range(slots):
            c = col_2[0, k, tile]
            p = c // (2 * span) * span + lax.rem(c, span)
            g = p // (2 * tiles) * tiles + lax.rem(p, tiles)
            hots = columns(col_2, m2v, pairs2, tile, k, tiles, g)
            sub_copy(i, k).wait_recv()
            fin_a[i, k] = merged([lev_a[0, i, k]], [lev_a[1, i, k]], rows, [hots])[0]

    feat_near.wait()
    for i in range(quarter):
        tile = 4 * i + 2 * b + s
        rows = turned(m2v[pl.ds(first_group + tile, 1), :], width)
        at = pl.ds(i * width, width)
        total = lev_f[0, :, at].astype(jnp.float32) + right_side(lev_f[1, :, at], rows)
        fin_f[:, at] = total.astype(jnp.bfloat16)

    @pl.loop(0, quarter)
    def _(i):
        for q in range(groups):
            core_copy(0, i, q).wait_send()
            core_copy(1, i, q).wait_send()
        for k in range(slots):
            sub_copy(i, k).wait_send()


def put(tiles, feats, out_a, out_f, sem):
    copies = [
        pltpu.make_async_copy(tiles, out_a, sem.at[0]),
        pltpu.make_async_copy(feats, out_f, sem.at[1]),
    ]
    for copy in copies:
        copy.start()
    for copy in copies:
        copy.wait()


def per_device(features, adjacency, col_tiles, match_one, match_two):
    tiles, slots, width = adjacency.shape[:3]
    feats = features.shape[0]
    quarter, groups = tiles // 4, slots // GROUP
    span = lax.axis_size("sub") * tiles
    half = jnp.bfloat16

    def outside(part):
        return pltpu.with_memory_space_constraint(part, pltpu.HBM)

    dma = pltpu.SemaphoreType.DMA
    anywhere = pl.BlockSpec(memory_space=pltpu.HBM)
    inside = pl.BlockSpec(memory_space=pltpu.VMEM)
    tile_out = ((quarter, slots, width, width), half)
    feat_out = ((feats, quarter * width), half)
    done = pl.pallas_call(
        functools.partial(kernel, span),
        out_shape=(pltpu.VMEM(*tile_out), pltpu.VMEM(*feat_out)),
        in_specs=[anywhere] * 5,
        out_specs=(inside, inside),
        scratch_shapes=[
            pltpu.VMEM((match_one.shape[0] + 8, width), jnp.int32),
            pltpu.VMEM((match_two.shape[0] + 8, width), jnp.int32),
            pltpu.SMEM((2, slots, tiles), jnp.int32),
            pltpu.SMEM((2, slots, tiles), jnp.int32),
            pltpu.VMEM((2, 2, quarter, slots, width, width), half),
            pltpu.VMEM((2,) + features.shape, half),
            pltpu.VMEM((quarter, slots, width, width), half),
            pltpu.VMEM((feats, quarter * width), half),
            pltpu.VMEM((2, quarter, slots, width, width), half),
            pltpu.VMEM((2, feats, quarter * width), half),
            dma((5,)),
            dma((2, quarter, groups)),
            dma((2, quarter, groups)),
            dma((2, quarter, groups)),
            dma((quarter, slots)),
            dma((quarter, slots)),
            dma((4,)),
            dma((4,)),
        ],
        compiler_params=pltpu.CompilerParams(
            collective_id=0, has_side_effects=True, vmem_limit_bytes=VMEM_BYTES
        ),
        name="coarsen",
    )(*(outside(part) for part in (features, adjacency, col_tiles.T, match_one, match_two)))
    return pl.pallas_call(
        put,
        out_shape=(jax.ShapeDtypeStruct(*tile_out), jax.ShapeDtypeStruct(*feat_out)),
        in_specs=[inside] * 2,
        out_specs=(anywhere, anywhere),
        scratch_shapes=[dma((2,))],
        name="put",
    )(*(pltpu.with_memory_space_constraint(part, pltpu.VMEM) for part in done))


def solution(mesh):
    placed = (
        P(None, ("blk", "sub")),
        P(("blk", "sub"), None, None, None),
        P(("blk", "sub"), None),
        P(),
        P(),
    )
    return jax.shard_map(
        per_device,
        mesh=mesh,
        in_specs=placed,
        out_specs=(P(("blk", "sub"), None, None, None), P(None, ("blk", "sub"))),
        check_vma=False,
    )
```

```python
import functools

import jax
import jax.numpy as jnp
from jax import lax
from jax.experimental import pallas as pl
from jax.experimental.pallas import tpu as pltpu
from jax.sharding import PartitionSpec as P

MESH = pl.DeviceIdType.MESH
GROUP = 2
LAST = (0, 0, 0, 0, 1, 1, 2, 3)
VMEM_BYTES = 24 * 2**20


def turned(row_map, width):
    down = lax.broadcasted_iota(jnp.int32, (width, width), 0)
    return jnp.where(down == row_map, 1.0, 0.0).astype(jnp.bfloat16)


def right_side(blocks, turned_hot):
    return lax.dot_general(
        blocks, turned_hot, (((1,), (1,)), ((), ())), preferred_element_type=jnp.float32
    )


def merged(low, high, turned_rows, turned_cols):
    width = turned_rows.shape[0]
    moved = jnp.dot(
        turned_rows, jnp.concatenate(high, axis=1), preferred_element_type=jnp.float32
    ).astype(jnp.bfloat16)
    out = []
    for n, block in enumerate(low):
        both = jnp.concatenate([block, moved[:, n * width : (n + 1) * width]], axis=1)
        out.append(right_side(both, turned_cols[n]).astype(jnp.bfloat16))
    return out


def kernel(
    span, feat, adj, cols, m1, m2, fin_a, fin_f,
    m1v, m2v, col_1, col_2, adj_v, feat_v, send_a, send_f, lev_a, lev_f,
    loc_sem, own_sem, cr_sem, sr_sem, send_sem, xr_sem,
):
    tiles, slots, width = adj.shape[0], adj.shape[1], adj.shape[2]
    quarter = tiles // 4
    groups = slots // GROUP
    blk, sub = lax.axis_index("blk"), lax.axis_index("sub")
    b, s = lax.rem(blk, 2), lax.rem(sub, 2)
    core = {"blk": blk + 1 - 2 * b}
    near = {"sub": sub + 1 - 2 * s}
    subs = span // tiles
    first_pair = (blk // 2 * subs + sub) * tiles
    first_group = (blk // 2 * (subs // 2) + sub // 2) * tiles
    pairs, pairs2 = m1.shape[0], m2.shape[0]

    def side(j):
        return (1 - s) * (1 - j) + s * j

    def own_copy(j, i, part, n):
        return pltpu.make_async_copy(
            adj.at[4 * i + 2 * b + side(j), part], adj_v.at[b, j, i, part], own_sem.at[n]
        )

    def core_copy(j, i, part, n):
        return pltpu.make_async_remote_copy(
            src_ref=adj.at[4 * i + 2 * (1 - b) + side(j), part],
            dst_ref=adj_v.at[b, j, i, part],
            send_sem=send_sem.at[0], recv_sem=cr_sem.at[n],
            device_id=core, device_id_type=MESH,
        )

    def sub_copy(i, k, n):
        return pltpu.make_async_remote_copy(
            src_ref=send_a.at[i, k], dst_ref=lev_a.at[s, i, k],
            send_sem=send_sem.at[1], recv_sem=sr_sem.at[n],
            device_id=near, device_id_type=MESH,
        )

    def small(src, dst, n, device):
        return pltpu.make_async_remote_copy(
            src_ref=src, dst_ref=dst, send_sem=send_sem.at[2 + n], recv_sem=xr_sem.at[n],
            device_id=device, device_id_type=MESH,
        )

    def all_of(ref, sem):
        pltpu.make_async_copy(ref, ref, sem).wait()

    barrier = pltpu.get_barrier_semaphore()
    pl.semaphore_signal(barrier, inc=1, device_id=core, device_id_type=MESH)
    pl.semaphore_signal(barrier, inc=1, device_id=near, device_id_type=MESH)

    local = [
        pltpu.make_async_copy(m1, m1v.at[pl.ds(0, pairs)], loc_sem.at[0]),
        pltpu.make_async_copy(cols, col_1.at[b], loc_sem.at[1]),
        pltpu.make_async_copy(cols, col_2.at[s], loc_sem.at[2]),
        pltpu.make_async_copy(feat, feat_v.at[b], loc_sem.at[3]),
        pltpu.make_async_copy(m2, m2v.at[pl.ds(0, pairs2)], loc_sem.at[4]),
    ]
    for n in range(3):
        local[n].start()
    whole = pl.ds(0, slots)
    first = [pl.ds(q * GROUP, GROUP) for q in range(groups)]
    last = quarter - 1
    for q in range(groups):
        own_copy(0, 0, first[q], q).start()

    plain = lax.broadcasted_iota(jnp.int32, (8, width), 1)
    m1v[pl.ds(pairs, 8), :] = plain
    m2v[pl.ds(pairs2, 8), :] = plain

    pl.semaphore_wait(barrier, 2)
    cols_core = small(cols, col_1.at[b], 0, core)
    cols_near = small(cols, col_2.at[s], 1, near)
    feat_core = small(feat, feat_v.at[b], 2, core)
    cols_core.start()
    for q in range(groups):
        core_copy(0, 0, first[q], q).start()
    feat_core.start()
    cols_near.start()
    local[3].start()

    @pl.loop(1, quarter)
    def _(i):
        core_copy(0, i, whole, groups - 1 + i).start()
        own_copy(0, i, whole, groups - 1 + i).start()

    @pl.loop(0, quarter)
    def _(i):
        core_copy(1, i, whole, groups - 1 + quarter + i).start()
        own_copy(1, i, whole, groups - 1 + quarter + i).start()

    local[4].start()

    for n in range(3):
        local[n].wait()
    cols_core.wait_recv()

    def columns(table, maps, plain_row, tile, k, bit, row):
        hots = []
        for part in range(2):
            upper = lax.rem(table[part, k, tile] // bit, 2)
            here = maps[pl.ds(upper * row + (1 - upper) * plain_row, 1), :]
            hots.append(turned(here, width))
        return jnp.concatenate(hots, axis=1)

    def first_rows(tile):
        return turned(m1v[pl.ds(first_pair + tile, 1), :], width)

    def first_level(j, i, store, parts):
        tile = 4 * i + 2 * b + side(j)
        rows = first_rows(tile)
        for q in range(groups):
            for part, n in parts.get(q, ()):
                own_copy(j, i, part, n).wait()
                core_copy(j, i, part, n).wait_recv()
            ks = range(q * GROUP, (q + 1) * GROUP)
            hots = []
            for k in ks:
                c = col_1[0, k, tile]
                p = c // (2 * span) * span + lax.rem(c, span)
                hots.append(columns(col_1, m1v, pairs, tile, k, span, p))
            done = merged(
                [adj_v[0, j, i, k] for k in ks], [adj_v[1, j, i, k] for k in ks], rows, hots
            )
            store(i, ks, done)
        return tile, rows

    def feature_level(j, i, tile, rows, dst):
        at = pl.ds(pl.multiple_of(tile * width, width), width)
        total = feat_v[0, :, at].astype(jnp.float32) + right_side(feat_v[1, :, at], rows)
        dst[:, pl.ds(pl.multiple_of(i * width, width), width)] = total.astype(jnp.bfloat16)

    def store_send(arrival):
        def store(i, ks, done):
            for k, block in zip(ks, done):
                send_a[i, k] = block
                sub_copy(i, k, arrival(i, k)).start()

        return store

    def store_keep(i, ks, done):
        for k, block in zip(ks, done):
            lev_a[s, i, k] = block

    def last_arrival(i, k):
        return last + LAST[k]

    first_level(0, 0, store_send(lambda i, k: 0), {q: [(first[q], q)] for q in range(groups)})

    local[3].wait()
    feat_core.wait_recv()
    for i in range(quarter):
        tile = 4 * i + 2 * b + side(0)
        feature_level(0, i, tile, first_rows(tile), send_f)
    feat_near = small(send_f, lev_f.at[s], 3, near)
    feat_near.start()

    @pl.loop(1, last)
    def _(i):
        first_level(0, i, store_send(lambda i, k: i), {0: [(whole, groups - 1 + i)]})

    first_level(0, last, store_send(last_arrival), {0: [(whole, groups - 1 + last)]})

    @pl.loop(0, quarter)
    def _(i):
        tile, rows = first_level(1, i, store_keep, {0: [(whole, groups - 1 + quarter + i)]})
        feature_level(1, i, tile, rows, lev_f.at[s])

    local[4].wait()
    cols_near.wait_recv()

    def second_rows(tile):
        return turned(m2v[pl.ds(first_group + tile, 1), :], width)

    def second_level(i, waits):
        tile = 4 * i + 2 * b + s
        rows = second_rows(tile)
        for k in range(slots):
            c = col_2[0, k, tile]
            p = c // (2 * span) * span + lax.rem(c, span)
            g = p // (2 * tiles) * tiles + lax.rem(p, tiles)
            hots = columns(col_2, m2v, pairs2, tile, k, tiles, g)
            if k in waits:
                count, n = waits[k]
                all_of(lev_a.at[1 - s, i, pl.ds(k, count)], sr_sem.at[n])
            fin_a[i, k] = merged([lev_a[0, i, k]], [lev_a[1, i, k]], rows, [hots])[0]

    @pl.loop(0, last)
    def _(i):
        second_level(i, {0: (slots, i)})

    feat_near.wait_recv()
    for i in range(quarter):
        at = pl.ds(i * width, width)
        rows = second_rows(4 * i + 2 * b + s)
        total = lev_f[0, :, at].astype(jnp.float32) + right_side(lev_f[1, :, at], rows)
        fin_f[:, at] = total.astype(jnp.bfloat16)

    second_level(
        last, {LAST.index(n): (LAST.count(n), last + n) for n in range(max(LAST) + 1)}
    )

    all_of(adj_v.at[0], send_sem.at[0])
    all_of(send_a, send_sem.at[1])
    for copy in (cols_core, cols_near, feat_core, feat_near):
        copy.wait_send()


def put(tiles, feats, out_a, out_f, sem):
    copies = [
        pltpu.make_async_copy(tiles, out_a, sem.at[0]),
        pltpu.make_async_copy(feats, out_f, sem.at[1]),
    ]
    for copy in copies:
        copy.start()
    for copy in copies:
        copy.wait()


def per_device(features, adjacency, col_tiles, match_one, match_two):
    tiles, slots, width = adjacency.shape[:3]
    feats = features.shape[0]
    quarter, groups = tiles // 4, slots // GROUP
    span = lax.axis_size("sub") * tiles
    half = jnp.bfloat16

    def outside(part):
        return pltpu.with_memory_space_constraint(part, pltpu.HBM)

    dma = pltpu.SemaphoreType.DMA
    anywhere = pl.BlockSpec(memory_space=pltpu.HBM)
    inside = pl.BlockSpec(memory_space=pltpu.VMEM)
    tile_out = ((quarter, slots, width, width), half)
    feat_out = ((feats, quarter * width), half)
    done = pl.pallas_call(
        functools.partial(kernel, span),
        out_shape=(pltpu.VMEM(*tile_out), pltpu.VMEM(*feat_out)),
        in_specs=[anywhere] * 5,
        out_specs=(inside, inside),
        scratch_shapes=[
            pltpu.VMEM((match_one.shape[0] + 8, width), jnp.int32),
            pltpu.VMEM((match_two.shape[0] + 8, width), jnp.int32),
            pltpu.SMEM((2, slots, tiles), jnp.int32),
            pltpu.SMEM((2, slots, tiles), jnp.int32),
            pltpu.VMEM((2, 2, quarter, slots, width, width), half),
            pltpu.VMEM((2,) + features.shape, half),
            pltpu.VMEM((quarter, slots, width, width), half),
            pltpu.VMEM((feats, quarter * width), half),
            pltpu.VMEM((2, quarter, slots, width, width), half),
            pltpu.VMEM((2, feats, quarter * width), half),
            dma((5,)),
            dma((groups - 1 + 2 * quarter,)),
            dma((groups - 1 + 2 * quarter,)),
            dma((quarter + max(LAST),)),
            dma((6,)),
            dma((4,)),
        ],
        compiler_params=pltpu.CompilerParams(
            collective_id=0, has_side_effects=True, vmem_limit_bytes=VMEM_BYTES
        ),
        name="coarsen",
    )(*(outside(part) for part in (features, adjacency, col_tiles.T, match_one, match_two)))
    return pl.pallas_call(
        put,
        out_shape=(jax.ShapeDtypeStruct(*tile_out), jax.ShapeDtypeStruct(*feat_out)),
        in_specs=[inside] * 2,
        out_specs=(anywhere, anywhere),
        scratch_shapes=[dma((2,))],
        name="put",
    )(*(pltpu.with_memory_space_constraint(part, pltpu.VMEM) for part in done))


def solution(mesh):
    placed = (
        P(None, ("blk", "sub")),
        P(("blk", "sub"), None, None, None),
        P(("blk", "sub"), None),
        P(),
        P(),
    )
    return jax.shard_map(
        per_device,
        mesh=mesh,
        in_specs=placed,
        out_specs=(P(("blk", "sub"), None, None, None), P(None, ("blk", "sub"))),
        check_vma=False,
    )
```

```python
import functools

import jax
import jax.numpy as jnp
from jax import lax
from jax.experimental import pallas as pl
from jax.experimental.pallas import tpu as pltpu
from jax.sharding import PartitionSpec as P

MESH = pl.DeviceIdType.MESH
GROUP = 2
LAST = (0, 0, 0, 0, 1, 1, 2, 3)
RAW = 1
LAG = 2
VMEM_BYTES = 24 * 2**20


def turned(row_map, width):
    down = lax.broadcasted_iota(jnp.int32, (width, width), 0)
    return jnp.where(down == row_map, 1.0, 0.0).astype(jnp.bfloat16)


def right_side(blocks, turned_hot):
    return lax.dot_general(
        blocks, turned_hot, (((1,), (1,)), ((), ())), preferred_element_type=jnp.float32
    )


def merged(low, high, turned_rows, turned_cols):
    width = turned_rows.shape[0]
    moved = jnp.dot(
        turned_rows, jnp.concatenate(high, axis=1), preferred_element_type=jnp.float32
    ).astype(jnp.bfloat16)
    out = []
    for n, block in enumerate(low):
        both = jnp.concatenate([block, moved[:, n * width : (n + 1) * width]], axis=1)
        out.append(right_side(both, turned_cols[n]).astype(jnp.bfloat16))
    return out


def kernel(
    span, feat, adj, cols, m1, m2, fin_a, fin_f,
    m1v, m2v, col_1, col_2, col_3, raw_v, adj_v, feat_v, send_a, send_f, lev_a, lev_f,
    loc_sem, got_sem, sr_sem, send_sem, xr_sem,
):
    tiles, slots, width = adj.shape[0], adj.shape[1], adj.shape[2]
    quarter = tiles // 4
    groups = slots // GROUP
    blk, sub = lax.axis_index("blk"), lax.axis_index("sub")
    b, s = lax.rem(blk, 2), lax.rem(sub, 2)
    core = {"blk": blk + 1 - 2 * b}
    near = {"sub": sub + 1 - 2 * s}
    across = {"blk": blk + 1 - 2 * b, "sub": sub + 1 - 2 * s}
    subs = span // tiles
    first_pair = (blk // 2 * subs + sub) * tiles
    first_group = (blk // 2 * (subs // 2) + sub // 2) * tiles
    pairs, pairs2 = m1.shape[0], m2.shape[0]

    def side(j):
        return (1 - s) * (1 - j) + s * j

    def own_copy(j, i, part, n):
        return pltpu.make_async_copy(
            adj.at[4 * i + 2 * b + side(j), part], adj_v.at[b, j, i, part], got_sem.at[n]
        )

    def core_copy(j, i, part, n):
        return pltpu.make_async_remote_copy(
            src_ref=adj.at[4 * i + 2 * (1 - b) + side(j), part],
            dst_ref=adj_v.at[b, j, i, part],
            send_sem=send_sem.at[0], recv_sem=got_sem.at[n],
            device_id=core, device_id_type=MESH,
        )

    def sub_copy(i, k, n):
        return pltpu.make_async_remote_copy(
            src_ref=send_a.at[i * slots + k], dst_ref=lev_a.at[s, i, k],
            send_sem=send_sem.at[1], recv_sem=sr_sem.at[n],
            device_id=near, device_id_type=MESH,
        )

    def small(src, dst, n, device):
        return pltpu.make_async_remote_copy(
            src_ref=src, dst_ref=dst, send_sem=send_sem.at[2 + n], recv_sem=xr_sem.at[n],
            device_id=device, device_id_type=MESH,
        )

    def all_of(ref, sem):
        pltpu.make_async_copy(ref, ref, sem).wait()

    barrier = pltpu.get_barrier_semaphore()
    pl.semaphore_signal(barrier, inc=1, device_id=core, device_id_type=MESH)
    pl.semaphore_signal(barrier, inc=1, device_id=near, device_id_type=MESH)
    pl.semaphore_signal(barrier, inc=1, device_id=across, device_id_type=MESH)

    local = [
        pltpu.make_async_copy(m1, m1v.at[pl.ds(0, pairs)], loc_sem.at[0]),
        pltpu.make_async_copy(cols, col_1.at[b], loc_sem.at[1]),
        pltpu.make_async_copy(cols, col_2.at[s], loc_sem.at[2]),
        pltpu.make_async_copy(feat, feat_v.at[b], loc_sem.at[3]),
        pltpu.make_async_copy(m2, m2v.at[pl.ds(0, pairs2)], loc_sem.at[4]),
    ]
    for n in range(3):
        local[n].start()
    whole = pl.ds(0, slots)
    first = [pl.ds(max(RAW, q * GROUP), (q + 1) * GROUP - max(RAW, q * GROUP)) for q in range(groups)]
    late = [q for q in range(groups) if (q + 1) * GROUP > RAW]
    last = quarter - 1
    for q in late:
        own_copy(0, 0, first[q], q).start()

    plain = lax.broadcasted_iota(jnp.int32, (8, width), 1)
    m1v[pl.ds(pairs, 8), :] = plain
    m2v[pl.ds(pairs2, 8), :] = plain

    pl.semaphore_wait(barrier, 3)
    cols_core = small(cols, col_1.at[b], 0, core)
    cols_near = small(cols, col_2.at[s], 1, near)
    feat_core = small(feat, feat_v.at[b], 2, core)
    cols_core.start()
    for q in late:
        core_copy(0, 0, first[q], q).start()
    early = pl.ds(0, RAW)
    raw_near = small(adj.at[2 * b + side(0), early], raw_v.at[b], 4, near)
    raw_across = small(adj.at[2 * (1 - b) + side(0), early], raw_v.at[b], 5, across)
    raw_near.start()
    raw_across.start()
    cols_across = small(cols, col_3, 6, across)
    feat_core.start()
    cols_near.start()
    cols_across.start()
    local[3].start()

    @pl.loop(1, quarter)
    def _(i):
        core_copy(0, i, whole, groups - 1 + i).start()
        own_copy(0, i, whole, groups - 1 + i).start()

    @pl.loop(0, quarter)
    def _(i):
        core_copy(1, i, whole, groups - 1 + quarter + i).start()
        own_copy(1, i, whole, groups - 1 + quarter + i).start()

    local[4].start()

    for n in range(3):
        local[n].wait()
    cols_core.wait_recv()

    def columns(table, maps, plain_row, tile, k, bit, row):
        hots = []
        for part in range(2):
            upper = lax.rem(table[part, k, tile] // bit, 2)
            here = maps[pl.ds(upper * row + (1 - upper) * plain_row, 1), :]
            hots.append(turned(here, width))
        return jnp.concatenate(hots, axis=1)

    def first_rows(tile):
        return turned(m1v[pl.ds(first_pair + tile, 1), :], width)

    def first_level(j, i, store, parts, start=0):
        tile = 4 * i + 2 * b + side(j)
        rows = first_rows(tile)
        for q in range(groups):
            for part, n in parts.get(q, ()):
                all_of(adj_v.at[:, j, i, part], got_sem.at[n])
            ks = range(max(start, q * GROUP), (q + 1) * GROUP)
            if not ks:
                continue
            hots = []
            for k in ks:
                c = col_1[0, k, tile]
                p = c // (2 * span) * span + lax.rem(c, span)
                hots.append(columns(col_1, m1v, pairs, tile, k, span, p))
            done = merged(
                [adj_v[0, j, i, k] for k in ks], [adj_v[1, j, i, k] for k in ks], rows, hots
            )
            store(i, ks, done)
        return tile, rows

    def feature_level(j, i, tile, rows, dst):
        at = pl.ds(pl.multiple_of(tile * width, width), width)
        total = feat_v[0, :, at].astype(jnp.float32) + right_side(feat_v[1, :, at], rows)
        dst[:, pl.ds(pl.multiple_of(i * width, width), width)] = total.astype(jnp.bfloat16)

    def arrival(i, k):
        return last + LAST[k] if isinstance(i, int) and i == last else i

    def store_send(i, ks, done):
        for k, block in zip(ks, done):
            send_a[i * slots + k] = block

        @pl.when(b == 1)
        def _():
            for k in ks:
                sub_copy(i, k, arrival(i, k)).start()

    def send_tile(i, begin):
        @pl.when(b == 0)
        def _():
            for k in range(begin, slots):
                sub_copy(i, k, arrival(i, k)).start()


    def store_keep(i, ks, done):
        for k, block in zip(ks, done):
            lev_a[s, i, k] = block

    first_level(0, 0, store_send, {q: [(first[q], q)] for q in late}, RAW)

    local[3].wait()
    feat_core.wait_recv()
    for i in range(quarter):
        tile = 4 * i + 2 * b + side(0)
        feature_level(0, i, tile, first_rows(tile), send_f)
    feat_near = small(send_f, lev_f.at[s], 3, near)
    feat_near.start()

    for i in range(1, quarter):
        first_level(0, i, store_send, {0: [(whole, groups - 1 + i)]})
        if i >= LAG:
            send_tile(i - LAG, RAW if i == LAG else 0)
    for i in range(quarter - LAG, quarter):
        send_tile(i, RAW if i == 0 else 0)

    @pl.loop(0, quarter)
    def _(i):
        tile, rows = first_level(1, i, store_keep, {0: [(whole, groups - 1 + quarter + i)]})
        feature_level(1, i, tile, rows, lev_f.at[s])

    local[4].wait()
    for copy in (cols_near, cols_across, raw_near, raw_across):
        copy.wait_recv()
    there = 2 * b + s
    near_pair = (blk // 2 * subs + sub + 1 - 2 * s) * tiles
    near_rows = turned(m1v[pl.ds(near_pair + there, 1), :], width)
    hots = []
    for k in range(RAW):
        c = col_2[1 - s, k, there]
        p = c // (2 * span) * span + lax.rem(c, span)
        mine = lax.rem(c // span, 2)
        other = lax.rem(col_3[k, there] // span, 2)
        parts = []
        for upper in (b * other + (1 - b) * mine, b * mine + (1 - b) * other):
            row = upper * p + (1 - upper) * pairs
            parts.append(turned(m1v[pl.ds(row, 1), :], width))
        hots.append(jnp.concatenate(parts, axis=1))
    done = merged(
        [raw_v[0, k] for k in range(RAW)], [raw_v[1, k] for k in range(RAW)], near_rows, hots
    )
    for k in range(RAW):
        lev_a[1 - s, 0, k] = done[k]

    def second_rows(tile):
        return turned(m2v[pl.ds(first_group + tile, 1), :], width)

    def second_level(i, waits):
        tile = 4 * i + 2 * b + s
        rows = second_rows(tile)
        for k in range(slots):
            c = col_2[0, k, tile]
            p = c // (2 * span) * span + lax.rem(c, span)
            g = p // (2 * tiles) * tiles + lax.rem(p, tiles)
            hots = columns(col_2, m2v, pairs2, tile, k, tiles, g)
            if k in waits:
                count, n = waits[k]
                all_of(lev_a.at[1 - s, i, pl.ds(k, count)], sr_sem.at[n])
            fin_a[i, k] = merged([lev_a[0, i, k]], [lev_a[1, i, k]], rows, [hots])[0]

    second_level(0, {RAW: (slots - RAW, 0)})

    @pl.loop(1, last)
    def _(i):
        second_level(i, {0: (slots, i)})

    feat_near.wait_recv()
    for i in range(quarter):
        at = pl.ds(i * width, width)
        rows = second_rows(4 * i + 2 * b + s)
        total = lev_f[0, :, at].astype(jnp.float32) + right_side(lev_f[1, :, at], rows)
        fin_f[:, at] = total.astype(jnp.bfloat16)

    second_level(
        last, {LAST.index(n): (LAST.count(n), last + n) for n in range(max(LAST) + 1)}
    )

    all_of(adj_v.at[0, 0, 0, pl.ds(RAW, slots - RAW)], send_sem.at[0])
    all_of(adj_v.at[0, 0, pl.ds(1, last)], send_sem.at[0])
    all_of(adj_v.at[0, 1], send_sem.at[0])
    all_of(send_a.at[pl.ds(RAW, quarter * slots - RAW)], send_sem.at[1])
    for copy in (cols_core, cols_near, cols_across, feat_core, feat_near, raw_near, raw_across):
        copy.wait_send()


def put(tiles, feats, out_a, out_f, sem):
    copies = [
        pltpu.make_async_copy(tiles, out_a, sem.at[0]),
        pltpu.make_async_copy(feats, out_f, sem.at[1]),
    ]
    for copy in copies:
        copy.start()
    for copy in copies:
        copy.wait()


def per_device(features, adjacency, col_tiles, match_one, match_two):
    tiles, slots, width = adjacency.shape[:3]
    feats = features.shape[0]
    quarter, groups = tiles // 4, slots // GROUP
    span = lax.axis_size("sub") * tiles
    half = jnp.bfloat16

    def outside(part):
        return pltpu.with_memory_space_constraint(part, pltpu.HBM)

    dma = pltpu.SemaphoreType.DMA
    anywhere = pl.BlockSpec(memory_space=pltpu.HBM)
    inside = pl.BlockSpec(memory_space=pltpu.VMEM)
    tile_out = ((quarter, slots, width, width), half)
    feat_out = ((feats, quarter * width), half)
    done = pl.pallas_call(
        functools.partial(kernel, span),
        out_shape=(pltpu.VMEM(*tile_out), pltpu.VMEM(*feat_out)),
        in_specs=[anywhere] * 5,
        out_specs=(inside, inside),
        scratch_shapes=[
            pltpu.VMEM((match_one.shape[0] + 8, width), jnp.int32),
            pltpu.VMEM((match_two.shape[0] + 8, width), jnp.int32),
            pltpu.SMEM((2, slots, tiles), jnp.int32),
            pltpu.SMEM((2, slots, tiles), jnp.int32),
            pltpu.SMEM((slots, tiles), jnp.int32),
            pltpu.VMEM((2, RAW, width, width), half),
            pltpu.VMEM((2, 2, quarter, slots, width, width), half),
            pltpu.VMEM((2,) + features.shape, half),
            pltpu.VMEM((quarter * slots, width, width), half),
            pltpu.VMEM((feats, quarter * width), half),
            pltpu.VMEM((2, quarter, slots, width, width), half),
            pltpu.VMEM((2, feats, quarter * width), half),
            dma((5,)),
            dma((groups - 1 + 2 * quarter,)),
            dma((quarter + max(LAST),)),
            dma((9,)),
            dma((7,)),
        ],
        compiler_params=pltpu.CompilerParams(
            collective_id=0, has_side_effects=True, vmem_limit_bytes=VMEM_BYTES
        ),
        name="coarsen",
    )(*(outside(part) for part in (features, adjacency, col_tiles.T, match_one, match_two)))
    return pl.pallas_call(
        put,
        out_shape=(jax.ShapeDtypeStruct(*tile_out), jax.ShapeDtypeStruct(*feat_out)),
        in_specs=[inside] * 2,
        out_specs=(anywhere, anywhere),
        scratch_shapes=[dma((2,))],
        name="put",
    )(*(pltpu.with_memory_space_constraint(part, pltpu.VMEM) for part in done))


def solution(mesh):
    placed = (
        P(None, ("blk", "sub")),
        P(("blk", "sub"), None, None, None),
        P(("blk", "sub"), None),
        P(),
        P(),
    )
    return jax.shard_map(
        per_device,
        mesh=mesh,
        in_specs=placed,
        out_specs=(P(("blk", "sub"), None, None, None), P(None, ("blk", "sub"))),
        check_vma=False,
    )
```

```python
import functools

import jax
import jax.numpy as jnp
from jax import lax
from jax.experimental import pallas as pl
from jax.experimental.pallas import tpu as pltpu
from jax.sharding import PartitionSpec as P

MESH = pl.DeviceIdType.MESH
GROUP = 2
LAST = (0, 0, 0, 0, 0, 0, 1, 2)
RAW = 1
LAG = 2
VMEM_BYTES = 24 * 2**20


def turned(row_map, width):
    down = lax.broadcasted_iota(jnp.int32, (width, width), 0)
    return jnp.where(down == row_map, 1.0, 0.0).astype(jnp.bfloat16)


def right_side(blocks, turned_hot):
    return lax.dot_general(
        blocks, turned_hot, (((1,), (1,)), ((), ())), preferred_element_type=jnp.float32
    )


def merged(low, high, turned_rows, turned_cols):
    width = turned_rows.shape[0]
    moved = jnp.dot(
        turned_rows, jnp.concatenate(high, axis=1), preferred_element_type=jnp.float32
    ).astype(jnp.bfloat16)
    out = []
    for n, block in enumerate(low):
        both = jnp.concatenate([block, moved[:, n * width : (n + 1) * width]], axis=1)
        out.append(right_side(both, turned_cols[n]).astype(jnp.bfloat16))
    return out


def carried(blocks, turned_rows, turned_cols):
    width = turned_rows.shape[0]
    moved = jnp.dot(
        turned_rows, jnp.concatenate(blocks, axis=1), preferred_element_type=jnp.float32
    ).astype(jnp.bfloat16)
    return [
        right_side(moved[:, n * width : (n + 1) * width], turned_cols[n]).astype(jnp.bfloat16)
        for n in range(len(blocks))
    ]


def kernel(
    span, feat, adj, cols, m1, m2, fin_a, fin_f,
    m1v, m2v, col_1, col_2, col_3, raw_v, adj_v, feat_v, send_a, send_f, lev_a, lev_f,
    loc_sem, got_sem, sr_sem, send_sem, xr_sem,
):
    tiles, slots, width = adj.shape[0], adj.shape[1], adj.shape[2]
    quarter = tiles // 4
    groups = slots // GROUP
    blk, sub = lax.axis_index("blk"), lax.axis_index("sub")
    b, s = lax.rem(blk, 2), lax.rem(sub, 2)
    core = {"blk": blk + 1 - 2 * b}
    near = {"sub": sub + 1 - 2 * s}
    across = {"blk": blk + 1 - 2 * b, "sub": sub + 1 - 2 * s}
    subs = span // tiles
    first_pair = (blk // 2 * subs + sub) * tiles
    first_group = (blk // 2 * (subs // 2) + sub // 2) * tiles
    pairs, pairs2 = m1.shape[0], m2.shape[0]

    def side(j):
        return (1 - s) * (1 - j) + s * j

    def own_copy(j, i, part, n):
        return pltpu.make_async_copy(
            adj.at[4 * i + 2 * b + side(j), part], adj_v.at[b, j, i, part], got_sem.at[n]
        )

    def core_copy(j, i, part, n):
        return pltpu.make_async_remote_copy(
            src_ref=adj.at[4 * i + 2 * (1 - b) + side(j), part],
            dst_ref=adj_v.at[b, j, i, part],
            send_sem=send_sem, recv_sem=got_sem.at[n],
            device_id=core, device_id_type=MESH,
        )

    def sub_copy(i, k, n):
        return pltpu.make_async_remote_copy(
            src_ref=send_a.at[i * slots + k], dst_ref=lev_a.at[s, i, k],
            send_sem=send_sem, recv_sem=sr_sem.at[n],
            device_id=near, device_id_type=MESH,
        )

    def small(src, dst, n, device):
        return pltpu.make_async_remote_copy(
            src_ref=src, dst_ref=dst, send_sem=send_sem, recv_sem=xr_sem.at[n],
            device_id=device, device_id_type=MESH,
        )

    def all_of(ref, sem):
        pltpu.make_async_copy(ref, ref, sem).wait()

    barrier = pltpu.get_barrier_semaphore()
    pl.semaphore_signal(barrier, inc=1, device_id=core, device_id_type=MESH)
    pl.semaphore_signal(barrier, inc=1, device_id=near, device_id_type=MESH)
    pl.semaphore_signal(barrier, inc=1, device_id=across, device_id_type=MESH)

    local = [
        pltpu.make_async_copy(m1, m1v.at[pl.ds(0, pairs)], loc_sem.at[0]),
        pltpu.make_async_copy(cols, col_1.at[b], loc_sem.at[1]),
        pltpu.make_async_copy(cols, col_2.at[s], loc_sem.at[2]),
        pltpu.make_async_copy(feat, feat_v.at[b], loc_sem.at[3]),
        pltpu.make_async_copy(m2, m2v.at[pl.ds(0, pairs2)], loc_sem.at[4]),
    ]
    for n in range(3):
        local[n].start()
    whole = pl.ds(0, slots)
    edges = (RAW, GROUP, 2 * GROUP, slots)
    first = [pl.ds(low, high - low) for low, high in zip(edges, edges[1:])]
    heads = len(first) - 1
    last = quarter - 1
    for q in range(heads + 1):
        own_copy(0, 0, first[q], q).start()

    plain = lax.broadcasted_iota(jnp.int32, (8, width), 1)
    m1v[pl.ds(pairs, 8), :] = plain
    m2v[pl.ds(pairs2, 8), :] = plain

    pl.semaphore_wait(barrier, 3)
    cols_core = small(cols, col_1.at[b], 0, core)
    cols_near = small(cols, col_2.at[s], 1, near)
    feat_core = small(feat, feat_v.at[b], 2, core)
    cols_core.start()
    for q in range(heads + 1):
        core_copy(0, 0, first[q], q).start()
    early = pl.ds(0, RAW)
    raw_near = small(adj.at[2 * b + side(0), early], raw_v.at[b], 4, near)
    raw_across = small(adj.at[2 * (1 - b) + side(0), early], raw_v.at[b], 5, across)
    raw_near.start()
    raw_across.start()
    cols_across = small(cols, col_3, 6, across)
    feat_core.start()
    cols_near.start()
    cols_across.start()
    local[3].start()

    core_copy(0, 1, whole, heads + 1).start()
    own_copy(0, 1, whole, heads + 1).start()


    for n in range(3):
        local[n].wait()
    cols_core.wait_recv()

    def columns(table, maps, plain_row, tile, k, bit, row):
        hots = []
        for part in range(2):
            upper = lax.rem(table[part, k, tile] // bit, 2)
            here = maps[pl.ds(upper * row + (1 - upper) * plain_row, 1), :]
            hots.append(turned(here, width))
        return jnp.concatenate(hots, axis=1)

    def first_rows(tile):
        return turned(m1v[pl.ds(first_pair + tile, 1), :], width)

    def first_level(j, i, store, parts, start=0):
        tile = 4 * i + 2 * b + side(j)
        rows = first_rows(tile)
        for q in range(groups):
            for part, n in parts.get(q, ()):
                all_of(adj_v.at[:, j, i, part], got_sem.at[n])
            ks = range(max(start, q * GROUP), (q + 1) * GROUP)
            if not ks:
                continue
            hots = []
            for k in ks:
                c = col_1[0, k, tile]
                p = c // (2 * span) * span + lax.rem(c, span)
                hots.append(columns(col_1, m1v, pairs, tile, k, span, p))
            done = merged(
                [adj_v[0, j, i, k] for k in ks], [adj_v[1, j, i, k] for k in ks], rows, hots
            )
            store(i, ks, done)
        return tile, rows

    def feature_level(j, i, tile, rows, dst):
        at = pl.ds(pl.multiple_of(tile * width, width), width)
        total = feat_v[0, :, at].astype(jnp.float32) + right_side(feat_v[1, :, at], rows)
        dst[:, pl.ds(pl.multiple_of(i * width, width), width)] = total.astype(jnp.bfloat16)

    def arrival(i, k):
        return last + LAST[k] if isinstance(i, int) and i == last else i

    def own_second(j, ks, done):
        tile = 4 * last + 2 * b + side(j)
        high = s * (first_group + tile) + (1 - s) * pairs2
        rows = turned(m2v[pl.ds(high, 1), :], width)
        hots = []
        for k in ks:
            c = col_2[s, k, tile]
            p = c // (2 * span) * span + lax.rem(c, span)
            g = p // (2 * tiles) * tiles + lax.rem(p, tiles)
            upper = lax.rem(c // tiles, 2)
            hots.append(turned(m2v[pl.ds(upper * g + (1 - upper) * pairs2, 1), :], width))
        return carried(done, rows, hots)

    def store_send(i, ks, done):
        if i == last:
            done = own_second(0, ks, done)
        for k, block in zip(ks, done):
            send_a[i * slots + k] = block

        @pl.when(b == 1)
        def _():
            for k in ks:
                sub_copy(i, k, arrival(i, k)).start()

    def send_tile(i, begin):
        @pl.when(b == 0)
        def _():
            for k in range(begin, slots):
                sub_copy(i, k, arrival(i, k)).start()


    def store_keep(i, ks, done):
        if isinstance(i, int):
            done = own_second(1, ks, done)
        for k, block in zip(ks, done):
            lev_a[s, i, k] = block

    first_level(0, 0, store_send, {q: [(first[q], q)] for q in range(heads + 1)}, RAW)

    @pl.loop(2, quarter)
    def _(i):
        core_copy(0, i, whole, heads + i).start()
        own_copy(0, i, whole, heads + i).start()

    @pl.loop(0, quarter)
    def _(i):
        core_copy(1, i, whole, heads + quarter + i).start()
        own_copy(1, i, whole, heads + quarter + i).start()

    local[4].start()
    local[3].wait()
    feat_core.wait_recv()
    for i in range(quarter):
        tile = 4 * i + 2 * b + side(0)
        feature_level(0, i, tile, first_rows(tile), send_f)
    feat_near = small(send_f, lev_f.at[s], 3, near)
    feat_near.start()

    for i in range(1, quarter):
        if i == last:
            local[4].wait()
        first_level(0, i, store_send, {0: [(whole, heads + i)]})
        if i >= LAG:
            send_tile(i - LAG, RAW if i == LAG else 0)
    for i in range(quarter - LAG, quarter):
        send_tile(i, RAW if i == 0 else 0)

    def keep(i):
        tile, rows = first_level(1, i, store_keep, {0: [(whole, heads + quarter + i)]})
        feature_level(1, i, tile, rows, lev_f.at[s])

    pl.loop(0, last)(keep)
    keep(last)

    for copy in (cols_near, cols_across, raw_near, raw_across):
        copy.wait_recv()
    there = 2 * b + s
    near_pair = (blk // 2 * subs + sub + 1 - 2 * s) * tiles
    near_rows = turned(m1v[pl.ds(near_pair + there, 1), :], width)
    hots = []
    for k in range(RAW):
        c = col_2[1 - s, k, there]
        p = c // (2 * span) * span + lax.rem(c, span)
        mine = lax.rem(c // span, 2)
        other = lax.rem(col_3[k, there] // span, 2)
        parts = []
        for upper in (b * other + (1 - b) * mine, b * mine + (1 - b) * other):
            row = upper * p + (1 - upper) * pairs
            parts.append(turned(m1v[pl.ds(row, 1), :], width))
        hots.append(jnp.concatenate(parts, axis=1))
    done = merged(
        [raw_v[0, k] for k in range(RAW)], [raw_v[1, k] for k in range(RAW)], near_rows, hots
    )
    for k in range(RAW):
        lev_a[1 - s, 0, k] = done[k]

    def second_rows(tile):
        return turned(m2v[pl.ds(first_group + tile, 1), :], width)

    def second_level(i, begin):
        tile = 4 * i + 2 * b + s
        rows = second_rows(tile)
        for k in range(slots):
            c = col_2[0, k, tile]
            p = c // (2 * span) * span + lax.rem(c, span)
            g = p // (2 * tiles) * tiles + lax.rem(p, tiles)
            hots = columns(col_2, m2v, pairs2, tile, k, tiles, g)
            if k == begin:
                all_of(lev_a.at[1 - s, i, pl.ds(k, slots - k)], sr_sem.at[i])
            fin_a[i, k] = merged([lev_a[0, i, k]], [lev_a[1, i, k]], rows, [hots])[0]

    second_level(0, RAW)

    @pl.loop(1, last)
    def _(i):
        second_level(i, 0)

    feat_near.wait_recv()
    for i in range(quarter):
        at = pl.ds(i * width, width)
        rows = second_rows(4 * i + 2 * b + s)
        total = lev_f[0, :, at].astype(jnp.float32) + right_side(lev_f[1, :, at], rows)
        fin_f[:, at] = total.astype(jnp.bfloat16)

    for n in range(max(LAST) + 1):
        part = pl.ds(LAST.index(n), LAST.count(n))
        all_of(lev_a.at[1 - s, last, part], sr_sem.at[last + n])
        total = lev_a[0, last, part].astype(jnp.float32) + lev_a[1, last, part].astype(jnp.float32)
        fin_a[last, part] = total.astype(jnp.bfloat16)

    all_of(adj_v.at[0, 0, 0, pl.ds(RAW, slots - RAW)], send_sem)
    all_of(adj_v.at[0, 0, pl.ds(1, last)], send_sem)
    all_of(adj_v.at[0, 1], send_sem)
    all_of(send_a.at[pl.ds(RAW, quarter * slots - RAW)], send_sem)
    for copy in (cols_core, cols_near, cols_across, feat_core, feat_near, raw_near, raw_across):
        copy.wait_send()


def put(tiles, feats, out_a, out_f, sem):
    copies = [
        pltpu.make_async_copy(tiles, out_a, sem.at[0]),
        pltpu.make_async_copy(feats, out_f, sem.at[1]),
    ]
    for copy in copies:
        copy.start()
    for copy in copies:
        copy.wait()


def per_device(features, adjacency, col_tiles, match_one, match_two):
    tiles, slots, width = adjacency.shape[:3]
    feats = features.shape[0]
    quarter, groups = tiles // 4, slots // GROUP
    span = lax.axis_size("sub") * tiles
    half = jnp.bfloat16

    def outside(part):
        return pltpu.with_memory_space_constraint(part, pltpu.HBM)

    dma = pltpu.SemaphoreType.DMA
    anywhere = pl.BlockSpec(memory_space=pltpu.HBM)
    inside = pl.BlockSpec(memory_space=pltpu.VMEM)
    tile_out = ((quarter, slots, width, width), half)
    feat_out = ((feats, quarter * width), half)
    done = pl.pallas_call(
        functools.partial(kernel, span),
        out_shape=(pltpu.VMEM(*tile_out), pltpu.VMEM(*feat_out)),
        in_specs=[anywhere] * 5,
        out_specs=(inside, inside),
        scratch_shapes=[
            pltpu.VMEM((match_one.shape[0] + 8, width), jnp.int32),
            pltpu.VMEM((match_two.shape[0] + 8, width), jnp.int32),
            pltpu.SMEM((2, slots, tiles), jnp.int32),
            pltpu.SMEM((2, slots, tiles), jnp.int32),
            pltpu.SMEM((slots, tiles), jnp.int32),
            pltpu.VMEM((2, RAW, width, width), half),
            pltpu.VMEM((2, 2, quarter, slots, width, width), half),
            pltpu.VMEM((2,) + features.shape, half),
            pltpu.VMEM((quarter * slots, width, width), half),
            pltpu.VMEM((feats, quarter * width), half),
            pltpu.VMEM((2, quarter, slots, width, width), half),
            pltpu.VMEM((2, feats, quarter * width), half),
            dma((5,)),
            dma((2 + 2 * quarter,)),
            dma((quarter + max(LAST),)),
            dma,
            dma((7,)),
        ],
        compiler_params=pltpu.CompilerParams(
            collective_id=0, has_side_effects=True, vmem_limit_bytes=VMEM_BYTES
        ),
        name="coarsen",
    )(*(outside(part) for part in (features, adjacency, col_tiles.T, match_one, match_two)))
    return pl.pallas_call(
        put,
        out_shape=(jax.ShapeDtypeStruct(*tile_out), jax.ShapeDtypeStruct(*feat_out)),
        in_specs=[inside] * 2,
        out_specs=(anywhere, anywhere),
        scratch_shapes=[dma((2,))],
        name="put",
    )(*(pltpu.with_memory_space_constraint(part, pltpu.VMEM) for part in done))


def solution(mesh):
    placed = (
        P(None, ("blk", "sub")),
        P(("blk", "sub"), None, None, None),
        P(("blk", "sub"), None),
        P(),
        P(),
    )
    return jax.shard_map(
        per_device,
        mesh=mesh,
        in_specs=placed,
        out_specs=(P(("blk", "sub"), None, None, None), P(None, ("blk", "sub"))),
        check_vma=False,
    )
```

```python
import functools

import jax
import jax.numpy as jnp
from jax import lax
from jax.experimental import pallas as pl
from jax.experimental.pallas import tpu as pltpu
from jax.sharding import PartitionSpec as P

MESH = pl.DeviceIdType.MESH
GROUP = 2
LAST = (0, 0, 0, 0, 0, 0, 1, 2)
RAW = 1
LAG = 2
VMEM_BYTES = 24 * 2**20


def turned(row_map, width):
    down = lax.broadcasted_iota(jnp.int32, (width, width), 0)
    return jnp.where(down == row_map, 1.0, 0.0).astype(jnp.bfloat16)


def right_side(blocks, turned_hot):
    return lax.dot_general(
        blocks, turned_hot, (((1,), (1,)), ((), ())), preferred_element_type=jnp.float32
    )


def merged(low, high, turned_rows, turned_cols):
    width = turned_rows.shape[0]
    moved = jnp.dot(
        turned_rows, jnp.concatenate(high, axis=1), preferred_element_type=jnp.float32
    ).astype(jnp.bfloat16)
    out = []
    for n, block in enumerate(low):
        both = jnp.concatenate([block, moved[:, n * width : (n + 1) * width]], axis=1)
        out.append(right_side(both, turned_cols[n]).astype(jnp.bfloat16))
    return out


def carried(blocks, turned_rows, turned_cols):
    width = turned_rows.shape[0]
    moved = jnp.dot(
        turned_rows, jnp.concatenate(blocks, axis=1), preferred_element_type=jnp.float32
    ).astype(jnp.bfloat16)
    return [
        right_side(moved[:, n * width : (n + 1) * width], turned_cols[n]).astype(jnp.bfloat16)
        for n in range(len(blocks))
    ]


def kernel(
    span, feat, adj, cols, m1, m2, fin_a, fin_f,
    m1v, m2v, tab, raw_v, adj_v, feat_v, send_a, send_f, lev_a, lev_f,
    loc_sem, got_sem, sr_sem, send_sem, xr_sem,
):
    tiles, slots, width = adj.shape[0], adj.shape[1], adj.shape[2]
    quarter = tiles // 4
    groups = slots // GROUP
    blk, sub = lax.axis_index("blk"), lax.axis_index("sub")
    b, s = lax.rem(blk, 2), lax.rem(sub, 2)
    core = {"blk": blk + 1 - 2 * b}
    near = {"sub": sub + 1 - 2 * s}
    across = {"blk": blk + 1 - 2 * b, "sub": sub + 1 - 2 * s}
    subs = span // tiles
    first_pair = (blk // 2 * subs + sub) * tiles
    first_group = (blk // 2 * (subs // 2) + sub // 2) * tiles
    pairs, pairs2 = m1.shape[0], m2.shape[0]

    def side(j):
        return (1 - s) * (1 - j) + s * j

    def own_copy(j, i, part, n):
        return pltpu.make_async_copy(
            adj.at[4 * i + 2 * b + side(j), part], adj_v.at[b, j, i, part], got_sem.at[n]
        )

    def core_copy(j, i, part, n):
        return pltpu.make_async_remote_copy(
            src_ref=adj.at[4 * i + 2 * (1 - b) + side(j), part],
            dst_ref=adj_v.at[b, j, i, part],
            send_sem=send_sem, recv_sem=got_sem.at[n],
            device_id=core, device_id_type=MESH,
        )

    def sub_copy(i, k, n):
        return pltpu.make_async_remote_copy(
            src_ref=send_a.at[i * slots + k], dst_ref=lev_a.at[s, i, k],
            send_sem=send_sem, recv_sem=sr_sem.at[n],
            device_id=near, device_id_type=MESH,
        )

    def small(src, dst, n, device):
        return pltpu.make_async_remote_copy(
            src_ref=src, dst_ref=dst, send_sem=send_sem, recv_sem=xr_sem.at[n],
            device_id=device, device_id_type=MESH,
        )

    def all_of(ref, sem):
        pltpu.make_async_copy(ref, ref, sem).wait()

    barrier = pltpu.get_barrier_semaphore()
    pl.semaphore_signal(barrier, inc=1, device_id=core, device_id_type=MESH)
    pl.semaphore_signal(barrier, inc=1, device_id=near, device_id_type=MESH)
    pl.semaphore_signal(barrier, inc=1, device_id=across, device_id_type=MESH)

    local = [
        pltpu.make_async_copy(m1, m1v.at[pl.ds(0, pairs)], loc_sem.at[0]),
        pltpu.make_async_copy(cols, tab.at[b], loc_sem.at[1]),
        pltpu.make_async_copy(m2, m2v.at[pl.ds(0, pairs2)], loc_sem.at[2]),
        pltpu.make_async_copy(feat, feat_v.at[b], xr_sem.at[2]),
    ]
    whole = pl.ds(0, slots)
    edges = (RAW, GROUP, 2 * GROUP, slots)
    first = [pl.ds(low, high - low) for low, high in zip(edges, edges[1:])]
    heads = len(first) - 1
    last = quarter - 1
    plain = lax.broadcasted_iota(jnp.int32, (8, width), 1)
    m1v[pl.ds(pairs, 8), :] = plain
    m2v[pl.ds(pairs2, 8), :] = plain

    pl.semaphore_wait(barrier, 3)
    early = pl.ds(0, RAW)
    cols_core = small(cols, tab.at[b], 0, core)
    cols_near = small(cols, tab.at[2], 1, near)
    cols_across = small(cols, tab.at[3], 3, across)
    feat_core = small(feat, feat_v.at[b], 2, core)
    raw_near = small(adj.at[2 * b + side(0), early], raw_v.at[b], 4, near)
    raw_across = small(adj.at[2 * (1 - b) + side(0), early], raw_v.at[b], 4, across)
    core_copy(0, 0, first[0], 0).start()
    cols_core.start()
    raw_near.start()
    raw_across.start()
    for n in range(2):
        local[n].start()
    own_copy(0, 0, first[0], 0).start()
    for q in range(1, heads + 1):
        core_copy(0, 0, first[q], q).start()
        own_copy(0, 0, first[q], q).start()
    feat_core.start()
    cols_near.start()
    cols_across.start()
    local[3].start()

    core_copy(0, 1, whole, 3).start()
    own_copy(0, 1, whole, 3).start()


    local[0].wait()
    local[1].wait()
    cols_core.wait_recv()

    def columns(table, maps, plain_row, tile, k, bit, row):
        hots = []
        for part in range(2):
            upper = lax.rem(tab[table[part], k, tile] // bit, 2)
            here = maps[pl.ds(upper * row + (1 - upper) * plain_row, 1), :]
            hots.append(turned(here, width))
        return jnp.concatenate(hots, axis=1)

    def first_rows(tile):
        return turned(m1v[pl.ds(first_pair + tile, 1), :], width)

    def first_level(j, i, store, parts, start=0):
        tile = 4 * i + 2 * b + side(j)
        rows = first_rows(tile)
        for q in range(groups):
            for part, n in parts.get(q, ()):
                all_of(adj_v.at[:, j, i, part], got_sem.at[n])
            ks = range(max(start, q * GROUP), (q + 1) * GROUP)
            if not ks:
                continue
            hots = []
            for k in ks:
                c = tab[b, k, tile]
                p = c // (2 * span) * span + lax.rem(c, span)
                hots.append(columns((0, 1), m1v, pairs, tile, k, span, p))
            done = merged(
                [adj_v[0, j, i, k] for k in ks], [adj_v[1, j, i, k] for k in ks], rows, hots
            )
            store(i, ks, done)
        return tile, rows

    def feature_level(j, i, tile, rows, dst):
        at = pl.ds(pl.multiple_of(tile * width, width), width)
        total = feat_v[0, :, at].astype(jnp.float32) + right_side(feat_v[1, :, at], rows)
        dst[:, pl.ds(pl.multiple_of(i * width, width), width)] = total.astype(jnp.bfloat16)

    def arrival(i, k):
        return last + LAST[k] if isinstance(i, int) and i == last else i

    def own_second(j, ks, done):
        tile = 4 * last + 2 * b + side(j)
        high = s * (first_group + tile) + (1 - s) * pairs2
        rows = turned(m2v[pl.ds(high, 1), :], width)
        hots = []
        for k in ks:
            c = tab[b, k, tile]
            p = c // (2 * span) * span + lax.rem(c, span)
            g = p // (2 * tiles) * tiles + lax.rem(p, tiles)
            upper = lax.rem(c // tiles, 2)
            hots.append(turned(m2v[pl.ds(upper * g + (1 - upper) * pairs2, 1), :], width))
        return carried(done, rows, hots)

    def store_send(i, ks, done):
        if i == last:
            done = own_second(0, ks, done)
        for k, block in zip(ks, done):
            send_a[i * slots + k] = block

        @pl.when(b == 1)
        def _():
            for k in ks:
                sub_copy(i, k, arrival(i, k)).start()

    def send_tile(i, begin):
        @pl.when(b == 0)
        def _():
            for k in range(begin, slots):
                sub_copy(i, k, arrival(i, k)).start()


    def store_keep(i, ks, done):
        if isinstance(i, int):
            done = own_second(1, ks, done)
        for k, block in zip(ks, done):
            lev_a[s, i, k] = block

    first_level(0, 0, store_send, {q: [(first[q], q)] for q in range(heads + 1)}, RAW)

    @pl.loop(2, quarter)
    def _(i):
        core_copy(0, i, whole, 4).start()
        own_copy(0, i, whole, 4).start()

    @pl.loop(0, quarter)
    def _(i):
        core_copy(1, i, whole, 5).start()
        own_copy(1, i, whole, 5).start()

    local[2].start()
    all_of(feat_v, xr_sem.at[2])
    for i in range(quarter):
        tile = 4 * i + 2 * b + side(0)
        feature_level(0, i, tile, first_rows(tile), send_f)
    feat_near = small(send_f, lev_f.at[s], 5, near)
    feat_near.start()

    for i in range(1, quarter):
        if i == last:
            local[2].wait()
        if i == 2:
            all_of(adj_v.at[:, 0, pl.ds(2, quarter - 2)], got_sem.at[4])
        first_level(0, i, store_send, {0: [(whole, 3)]} if i == 1 else {})
        if i >= LAG:
            send_tile(i - LAG, RAW if i == LAG else 0)
    for i in range(quarter - LAG, quarter):
        send_tile(i, RAW if i == 0 else 0)

    def keep(i):
        tile, rows = first_level(1, i, store_keep, {})
        feature_level(1, i, tile, rows, lev_f.at[s])

    all_of(adj_v.at[:, 1], got_sem.at[5])
    pl.loop(0, last)(keep)
    keep(last)

    cols_near.wait_recv()
    cols_across.wait_recv()
    all_of(raw_v, xr_sem.at[4])
    there = 2 * b + s
    near_pair = (blk // 2 * subs + sub + 1 - 2 * s) * tiles
    near_rows = turned(m1v[pl.ds(near_pair + there, 1), :], width)
    hots = []
    for k in range(RAW):
        c = tab[2, k, there]
        p = c // (2 * span) * span + lax.rem(c, span)
        mine = lax.rem(c // span, 2)
        other = lax.rem(tab[3, k, there] // span, 2)
        parts = []
        for upper in (b * other + (1 - b) * mine, b * mine + (1 - b) * other):
            row = upper * p + (1 - upper) * pairs
            parts.append(turned(m1v[pl.ds(row, 1), :], width))
        hots.append(jnp.concatenate(parts, axis=1))
    done = merged(
        [raw_v[0, k] for k in range(RAW)], [raw_v[1, k] for k in range(RAW)], near_rows, hots
    )
    for k in range(RAW):
        lev_a[1 - s, 0, k] = done[k]

    def second_rows(tile):
        return turned(m2v[pl.ds(first_group + tile, 1), :], width)

    def second_level(i, begin):
        tile = 4 * i + 2 * b + s
        rows = second_rows(tile)
        for k in range(slots):
            c = tab[b, k, tile]
            p = c // (2 * span) * span + lax.rem(c, span)
            g = p // (2 * tiles) * tiles + lax.rem(p, tiles)
            hots = columns((b * (1 - s) + 2 * s, b * s + 2 * (1 - s)), m2v, pairs2, tile, k, tiles, g)
            if k == begin:
                all_of(lev_a.at[1 - s, i, pl.ds(k, slots - k)], sr_sem.at[i])
            fin_a[i, k] = merged([lev_a[0, i, k]], [lev_a[1, i, k]], rows, [hots])[0]

    second_level(0, RAW)

    @pl.loop(1, last)
    def _(i):
        second_level(i, 0)

    feat_near.wait_recv()
    for i in range(quarter):
        at = pl.ds(i * width, width)
        rows = second_rows(4 * i + 2 * b + s)
        total = lev_f[0, :, at].astype(jnp.float32) + right_side(lev_f[1, :, at], rows)
        fin_f[:, at] = total.astype(jnp.bfloat16)

    for n in range(max(LAST) + 1):
        part = pl.ds(LAST.index(n), LAST.count(n))
        all_of(lev_a.at[1 - s, last, part], sr_sem.at[last + n])
        total = lev_a[0, last, part].astype(jnp.float32) + lev_a[1, last, part].astype(jnp.float32)
        fin_a[last, part] = total.astype(jnp.bfloat16)

    all_of(adj_v.at[0, 0, 0, pl.ds(RAW, slots - RAW)], send_sem)
    all_of(adj_v.at[0, 0, pl.ds(1, last)], send_sem)
    all_of(adj_v.at[0, 1], send_sem)
    all_of(send_a.at[pl.ds(RAW, quarter * slots - RAW)], send_sem)
    for copy in (cols_core, cols_near, cols_across, feat_core, feat_near, raw_near, raw_across):
        copy.wait_send()


def put(tiles, feats, out_a, out_f, sem):
    copies = [
        pltpu.make_async_copy(tiles, out_a, sem.at[0]),
        pltpu.make_async_copy(feats, out_f, sem.at[1]),
    ]
    for copy in copies:
        copy.start()
    for copy in copies:
        copy.wait()


def per_device(features, adjacency, col_tiles, match_one, match_two):
    tiles, slots, width = adjacency.shape[:3]
    feats = features.shape[0]
    quarter, groups = tiles // 4, slots // GROUP
    span = lax.axis_size("sub") * tiles
    half = jnp.bfloat16

    def outside(part):
        return pltpu.with_memory_space_constraint(part, pltpu.HBM)

    dma = pltpu.SemaphoreType.DMA
    anywhere = pl.BlockSpec(memory_space=pltpu.HBM)
    inside = pl.BlockSpec(memory_space=pltpu.VMEM)
    tile_out = ((quarter, slots, width, width), half)
    feat_out = ((feats, quarter * width), half)
    done = pl.pallas_call(
        functools.partial(kernel, span),
        out_shape=(pltpu.VMEM(*tile_out), pltpu.VMEM(*feat_out)),
        in_specs=[anywhere] * 5,
        out_specs=(inside, inside),
        scratch_shapes=[
            pltpu.VMEM((match_one.shape[0] + 8, width), jnp.int32),
            pltpu.VMEM((match_two.shape[0] + 8, width), jnp.int32),
            pltpu.SMEM((4, slots, tiles), jnp.int32),
            pltpu.VMEM((2, RAW, width, width), half),
            pltpu.VMEM((2, 2, quarter, slots, width, width), half),
            pltpu.VMEM((2,) + features.shape, half),
            pltpu.VMEM((quarter * slots, width, width), half),
            pltpu.VMEM((feats, quarter * width), half),
            pltpu.VMEM((2, quarter, slots, width, width), half),
            pltpu.VMEM((2, feats, quarter * width), half),
            dma((3,)),
            dma((6,)),
            dma((quarter + max(LAST),)),
            dma,
            dma((6,)),
        ],
        compiler_params=pltpu.CompilerParams(
            collective_id=0, has_side_effects=True, vmem_limit_bytes=VMEM_BYTES
        ),
        name="coarsen",
    )(*(outside(part) for part in (features, adjacency, col_tiles.T, match_one, match_two)))
    return pl.pallas_call(
        put,
        out_shape=(jax.ShapeDtypeStruct(*tile_out), jax.ShapeDtypeStruct(*feat_out)),
        in_specs=[inside] * 2,
        out_specs=(anywhere, anywhere),
        scratch_shapes=[dma((2,))],
        name="put",
    )(*(pltpu.with_memory_space_constraint(part, pltpu.VMEM) for part in done))


def solution(mesh):
    placed = (
        P(None, ("blk", "sub")),
        P(("blk", "sub"), None, None, None),
        P(("blk", "sub"), None),
        P(),
        P(),
    )
    return jax.shard_map(
        per_device,
        mesh=mesh,
        in_specs=placed,
        out_specs=(P(("blk", "sub"), None, None, None), P(None, ("blk", "sub"))),
        check_vma=False,
    )
```

```python
import functools

import jax
import jax.numpy as jnp
from jax import lax
from jax.experimental import pallas as pl
from jax.experimental.pallas import tpu as pltpu
from jax.sharding import PartitionSpec as P

MESH = pl.DeviceIdType.MESH
GROUP = 2
LAST = (0, 0, 0, 0, 0, 0, 1, 2)
RAW = 1
LAG = 2
VMEM_BYTES = 24 * 2**20


def turned(row_map, width):
    down = lax.broadcasted_iota(jnp.int32, (width, width), 0)
    return jnp.where(down == row_map, 1.0, 0.0).astype(jnp.bfloat16)


def right_side(blocks, turned_hot):
    return lax.dot_general(
        blocks, turned_hot, (((1,), (1,)), ((), ())), preferred_element_type=jnp.float32
    )


def merged(low, high, turned_rows, turned_cols):
    width = turned_rows.shape[0]
    moved = jnp.dot(
        turned_rows, jnp.concatenate(high, axis=1), preferred_element_type=jnp.float32
    ).astype(jnp.bfloat16)
    out = []
    for n, block in enumerate(low):
        both = jnp.concatenate([block, moved[:, n * width : (n + 1) * width]], axis=1)
        out.append(right_side(both, turned_cols[n]).astype(jnp.bfloat16))
    return out


def carried(blocks, turned_rows, turned_cols):
    width = turned_rows.shape[0]
    moved = jnp.dot(
        turned_rows, jnp.concatenate(blocks, axis=1), preferred_element_type=jnp.float32
    ).astype(jnp.bfloat16)
    return [
        right_side(moved[:, n * width : (n + 1) * width], turned_cols[n]).astype(jnp.bfloat16)
        for n in range(len(blocks))
    ]


def kernel(
    span, feat, adj, cols, m1, m2, fin_a, fin_f,
    m1v, m2v, tab, raw_v, adj_v, feat_v, send_a, send_f, lev_a, lev_f,
    loc_sem, got_sem, sr_sem, send_sem, xr_sem,
):
    tiles, slots, width = adj.shape[0], adj.shape[1], adj.shape[2]
    quarter = tiles // 4
    groups = slots // GROUP
    blk, sub = lax.axis_index("blk"), lax.axis_index("sub")
    b, s = lax.rem(blk, 2), lax.rem(sub, 2)
    core = {"blk": blk + 1 - 2 * b}
    near = {"sub": sub + 1 - 2 * s}
    across = {"blk": blk + 1 - 2 * b, "sub": sub + 1 - 2 * s}
    subs = span // tiles
    first_pair = (blk // 2 * subs + sub) * tiles
    first_group = (blk // 2 * (subs // 2) + sub // 2) * tiles
    pairs, pairs2 = m1.shape[0], m2.shape[0]

    def side(j):
        return (1 - s) * (1 - j) + s * j

    def own_copy(j, i, part, n):
        return pltpu.make_async_copy(
            adj.at[4 * i + 2 * b + side(j), part], adj_v.at[b, j, i, part], got_sem.at[n]
        )

    def core_copy(j, i, part, n):
        return pltpu.make_async_remote_copy(
            src_ref=adj.at[4 * i + 2 * (1 - b) + side(j), part],
            dst_ref=adj_v.at[b, j, i, part],
            send_sem=send_sem, recv_sem=got_sem.at[n],
            device_id=core, device_id_type=MESH,
        )

    def sub_copy(i, k, n):
        return pltpu.make_async_remote_copy(
            src_ref=send_a.at[i * slots + k], dst_ref=lev_a.at[s, i, k],
            send_sem=send_sem, recv_sem=sr_sem.at[n],
            device_id=near, device_id_type=MESH,
        )

    def small(src, dst, n, device):
        return pltpu.make_async_remote_copy(
            src_ref=src, dst_ref=dst, send_sem=send_sem, recv_sem=xr_sem.at[n],
            device_id=device, device_id_type=MESH,
        )

    def all_of(ref, sem):
        pltpu.make_async_copy(ref, ref, sem).wait()

    barrier = pltpu.get_barrier_semaphore()
    pl.semaphore_signal(barrier, inc=1, device_id=core, device_id_type=MESH)
    pl.semaphore_signal(barrier, inc=1, device_id=near, device_id_type=MESH)
    pl.semaphore_signal(barrier, inc=1, device_id=across, device_id_type=MESH)

    local = [
        pltpu.make_async_copy(m1, m1v.at[pl.ds(0, pairs)], loc_sem.at[0]),
        pltpu.make_async_copy(cols, tab.at[b], loc_sem.at[1]),
        pltpu.make_async_copy(m2, m2v.at[pl.ds(0, pairs2)], loc_sem.at[2]),
        pltpu.make_async_copy(feat, feat_v.at[b], xr_sem.at[2]),
    ]
    whole = pl.ds(0, slots)
    edges = (RAW, GROUP, 2 * GROUP, slots)
    first = [pl.ds(low, high - low) for low, high in zip(edges, edges[1:])]
    heads = len(first) - 1
    last = quarter - 1
    plain = lax.broadcasted_iota(jnp.int32, (8, width), 1)
    m1v[pl.ds(pairs, 8), :] = plain
    m2v[pl.ds(pairs2, 8), :] = plain

    def load_first():
        local[1].start()
        for q in range(heads + 1):
            own_copy(0, 0, first[q], q).start()
        local[0].start()

    pl.when(b == 1)(load_first)
    pl.semaphore_wait(barrier, 3)
    early = pl.ds(0, RAW)
    cols_core = small(cols, tab.at[b], 0, core)
    cols_near = small(cols, tab.at[2], 1, near)
    cols_across = small(cols, tab.at[3], 3, across)
    feat_core = small(feat, feat_v.at[b], 2, core)
    raw_near = small(adj.at[2 * b + side(0), early], raw_v.at[b], 4, near)
    raw_across = small(adj.at[2 * (1 - b) + side(0), early], raw_v.at[b], 4, across)
    core_copy(0, 0, first[0], 0).start()
    cols_core.start()
    raw_near.start()
    raw_across.start()
    for q in range(1, heads + 1):
        core_copy(0, 0, first[q], q).start()
    pl.when(b == 0)(load_first)
    feat_core.start()
    cols_near.start()
    cols_across.start()
    local[3].start()

    core_copy(0, 1, whole, 3).start()
    own_copy(0, 1, whole, 3).start()


    local[0].wait()
    local[1].wait()
    cols_core.wait_recv()

    def columns(table, maps, plain_row, tile, k, bit, row):
        hots = []
        for part in range(2):
            upper = lax.rem(tab[table[part], k, tile] // bit, 2)
            here = maps[pl.ds(upper * row + (1 - upper) * plain_row, 1), :]
            hots.append(turned(here, width))
        return jnp.concatenate(hots, axis=1)

    def first_rows(tile):
        return turned(m1v[pl.ds(first_pair + tile, 1), :], width)

    def first_level(j, i, store, parts, start=0):
        tile = 4 * i + 2 * b + side(j)
        rows = first_rows(tile)
        for q in range(groups):
            for part, n in parts.get(q, ()):
                all_of(adj_v.at[:, j, i, part], got_sem.at[n])
            ks = range(max(start, q * GROUP), (q + 1) * GROUP)
            if not ks:
                continue
            hots = []
            for k in ks:
                c = tab[b, k, tile]
                p = c // (2 * span) * span + lax.rem(c, span)
                hots.append(columns((0, 1), m1v, pairs, tile, k, span, p))
            done = merged(
                [adj_v[0, j, i, k] for k in ks], [adj_v[1, j, i, k] for k in ks], rows, hots
            )
            store(i, ks, done)
        return tile, rows

    def feature_level(j, i, tile, rows, dst):
        at = pl.ds(pl.multiple_of(tile * width, width), width)
        total = feat_v[0, :, at].astype(jnp.float32) + right_side(feat_v[1, :, at], rows)
        dst[:, pl.ds(pl.multiple_of(i * width, width), width)] = total.astype(jnp.bfloat16)

    def arrival(i, k):
        return last + LAST[k] if isinstance(i, int) and i == last else i

    def own_second(j, ks, done):
        tile = 4 * last + 2 * b + side(j)
        high = s * (first_group + tile) + (1 - s) * pairs2
        rows = turned(m2v[pl.ds(high, 1), :], width)
        hots = []
        for k in ks:
            c = tab[b, k, tile]
            p = c // (2 * span) * span + lax.rem(c, span)
            g = p // (2 * tiles) * tiles + lax.rem(p, tiles)
            upper = lax.rem(c // tiles, 2)
            hots.append(turned(m2v[pl.ds(upper * g + (1 - upper) * pairs2, 1), :], width))
        return carried(done, rows, hots)

    def store_send(i, ks, done):
        if i == last:
            done = own_second(0, ks, done)
        for k, block in zip(ks, done):
            send_a[i * slots + k] = block

        @pl.when(b == 1)
        def _():
            for k in ks:
                sub_copy(i, k, arrival(i, k)).start()

    def send_tile(i, begin):
        @pl.when(b == 0)
        def _():
            for k in range(begin, slots):
                sub_copy(i, k, arrival(i, k)).start()


    def store_keep(i, ks, done):
        if isinstance(i, int):
            done = own_second(1, ks, done)
        for k, block in zip(ks, done):
            lev_a[s, i, k] = block

    first_level(0, 0, store_send, {q: [(first[q], q)] for q in range(heads + 1)}, RAW)

    @pl.loop(2, quarter)
    def _(i):
        core_copy(0, i, whole, 4).start()
        own_copy(0, i, whole, 4).start()

    @pl.loop(0, quarter)
    def _(i):
        core_copy(1, i, whole, 5).start()
        own_copy(1, i, whole, 5).start()

    local[2].start()
    all_of(feat_v, xr_sem.at[2])
    for i in range(quarter):
        tile = 4 * i + 2 * b + side(0)
        feature_level(0, i, tile, first_rows(tile), send_f)
    feat_near = small(send_f, lev_f.at[s], 5, near)
    feat_near.start()

    for i in range(1, quarter):
        if i == last:
            local[2].wait()
        if i == 2:
            all_of(adj_v.at[:, 0, pl.ds(2, quarter - 2)], got_sem.at[4])
        first_level(0, i, store_send, {0: [(whole, 3)]} if i == 1 else {})
        if i >= LAG:
            send_tile(i - LAG, RAW if i == LAG else 0)
    for i in range(quarter - LAG, quarter):
        send_tile(i, RAW if i == 0 else 0)

    def keep(i):
        tile, rows = first_level(1, i, store_keep, {})
        feature_level(1, i, tile, rows, lev_f.at[s])

    all_of(adj_v.at[:, 1], got_sem.at[5])
    pl.loop(0, last)(keep)
    keep(last)

    cols_near.wait_recv()
    cols_across.wait_recv()
    all_of(raw_v, xr_sem.at[4])
    there = 2 * b + s
    near_pair = (blk // 2 * subs + sub + 1 - 2 * s) * tiles
    near_rows = turned(m1v[pl.ds(near_pair + there, 1), :], width)
    hots = []
    for k in range(RAW):
        c = tab[2, k, there]
        p = c // (2 * span) * span + lax.rem(c, span)
        mine = lax.rem(c // span, 2)
        other = lax.rem(tab[3, k, there] // span, 2)
        parts = []
        for upper in (b * other + (1 - b) * mine, b * mine + (1 - b) * other):
            row = upper * p + (1 - upper) * pairs
            parts.append(turned(m1v[pl.ds(row, 1), :], width))
        hots.append(jnp.concatenate(parts, axis=1))
    done = merged(
        [raw_v[0, k] for k in range(RAW)], [raw_v[1, k] for k in range(RAW)], near_rows, hots
    )
    for k in range(RAW):
        lev_a[1 - s, 0, k] = done[k]

    def second_rows(tile):
        return turned(m2v[pl.ds(first_group + tile, 1), :], width)

    def second_level(i, begin):
        tile = 4 * i + 2 * b + s
        rows = second_rows(tile)
        for k in range(slots):
            c = tab[b, k, tile]
            p = c // (2 * span) * span + lax.rem(c, span)
            g = p // (2 * tiles) * tiles + lax.rem(p, tiles)
            hots = columns((b * (1 - s) + 2 * s, b * s + 2 * (1 - s)), m2v, pairs2, tile, k, tiles, g)
            if k == begin:
                all_of(lev_a.at[1 - s, i, pl.ds(k, slots - k)], sr_sem.at[i])
            fin_a[i, k] = merged([lev_a[0, i, k]], [lev_a[1, i, k]], rows, [hots])[0]

    second_level(0, RAW)

    @pl.loop(1, last)
    def _(i):
        second_level(i, 0)

    feat_near.wait_recv()
    for i in range(quarter):
        at = pl.ds(i * width, width)
        rows = second_rows(4 * i + 2 * b + s)
        total = lev_f[0, :, at].astype(jnp.float32) + right_side(lev_f[1, :, at], rows)
        fin_f[:, at] = total.astype(jnp.bfloat16)

    for n in range(max(LAST) + 1):
        part = pl.ds(LAST.index(n), LAST.count(n))
        all_of(lev_a.at[1 - s, last, part], sr_sem.at[last + n])
        total = lev_a[0, last, part].astype(jnp.float32) + lev_a[1, last, part].astype(jnp.float32)
        fin_a[last, part] = total.astype(jnp.bfloat16)

    all_of(adj_v.at[0, 0, 0, pl.ds(RAW, slots - RAW)], send_sem)
    all_of(adj_v.at[0, 0, pl.ds(1, last)], send_sem)
    all_of(adj_v.at[0, 1], send_sem)
    all_of(send_a.at[pl.ds(RAW, quarter * slots - RAW)], send_sem)
    for copy in (cols_core, cols_near, cols_across, feat_core, feat_near, raw_near, raw_across):
        copy.wait_send()


def put(tiles, feats, out_a, out_f, sem):
    copies = [
        pltpu.make_async_copy(tiles, out_a, sem.at[0]),
        pltpu.make_async_copy(feats, out_f, sem.at[1]),
    ]
    for copy in copies:
        copy.start()
    for copy in copies:
        copy.wait()


def per_device(features, adjacency, col_tiles, match_one, match_two):
    tiles, slots, width = adjacency.shape[:3]
    feats = features.shape[0]
    quarter, groups = tiles // 4, slots // GROUP
    span = lax.axis_size("sub") * tiles
    half = jnp.bfloat16

    def outside(part):
        return pltpu.with_memory_space_constraint(part, pltpu.HBM)

    dma = pltpu.SemaphoreType.DMA
    anywhere = pl.BlockSpec(memory_space=pltpu.HBM)
    inside = pl.BlockSpec(memory_space=pltpu.VMEM)
    tile_out = ((quarter, slots, width, width), half)
    feat_out = ((feats, quarter * width), half)
    done = pl.pallas_call(
        functools.partial(kernel, span),
        out_shape=(pltpu.VMEM(*tile_out), pltpu.VMEM(*feat_out)),
        in_specs=[anywhere] * 5,
        out_specs=(inside, inside),
        scratch_shapes=[
            pltpu.VMEM((match_one.shape[0] + 8, width), jnp.int32),
            pltpu.VMEM((match_two.shape[0] + 8, width), jnp.int32),
            pltpu.SMEM((4, slots, tiles), jnp.int32),
            pltpu.VMEM((2, RAW, width, width), half),
            pltpu.VMEM((2, 2, quarter, slots, width, width), half),
            pltpu.VMEM((2,) + features.shape, half),
            pltpu.VMEM((quarter * slots, width, width), half),
            pltpu.VMEM((feats, quarter * width), half),
            pltpu.VMEM((2, quarter, slots, width, width), half),
            pltpu.VMEM((2, feats, quarter * width), half),
            dma((3,)),
            dma((6,)),
            dma((quarter + max(LAST),)),
            dma,
            dma((6,)),
        ],
        compiler_params=pltpu.CompilerParams(
            collective_id=0, has_side_effects=True, vmem_limit_bytes=VMEM_BYTES
        ),
        name="coarsen",
    )(*(outside(part) for part in (features, adjacency, col_tiles.T, match_one, match_two)))
    return pl.pallas_call(
        put,
        out_shape=(jax.ShapeDtypeStruct(*tile_out), jax.ShapeDtypeStruct(*feat_out)),
        in_specs=[inside] * 2,
        out_specs=(anywhere, anywhere),
        scratch_shapes=[dma((2,))],
        name="put",
    )(*(pltpu.with_memory_space_constraint(part, pltpu.VMEM) for part in done))


def solution(mesh):
    placed = (
        P(None, ("blk", "sub")),
        P(("blk", "sub"), None, None, None),
        P(("blk", "sub"), None),
        P(),
        P(),
    )
    return jax.shard_map(
        per_device,
        mesh=mesh,
        in_specs=placed,
        out_specs=(P(("blk", "sub"), None, None, None), P(None, ("blk", "sub"))),
        check_vma=False,
    )
```

```python
import functools

import jax
import jax.numpy as jnp
from jax import lax
from jax.experimental import pallas as pl
from jax.experimental.pallas import tpu as pltpu
from jax.sharding import PartitionSpec as P

MESH = pl.DeviceIdType.MESH
GROUP = 2
LAST = (0, 0, 0, 0, 0, 0, 1, 2)
RAW = 1
LAG = 2
VMEM_BYTES = 24 * 2**20


def turned(row_map, width):
    down = lax.broadcasted_iota(jnp.int32, (width, width), 0)
    return jnp.where(down == row_map, 1.0, 0.0).astype(jnp.bfloat16)


def right_side(blocks, turned_hot):
    return lax.dot_general(
        blocks, turned_hot, (((1,), (1,)), ((), ())), preferred_element_type=jnp.float32
    )


def merged(low, high, turned_rows, turned_cols):
    width = turned_rows.shape[0]
    moved = jnp.dot(
        turned_rows, jnp.concatenate(high, axis=1), preferred_element_type=jnp.float32
    ).astype(jnp.bfloat16)
    out = []
    for n, block in enumerate(low):
        both = jnp.concatenate([block, moved[:, n * width : (n + 1) * width]], axis=1)
        out.append(right_side(both, turned_cols[n]).astype(jnp.bfloat16))
    return out


def carried(blocks, turned_rows, turned_cols):
    width = turned_rows.shape[0]
    moved = jnp.dot(
        turned_rows, jnp.concatenate(blocks, axis=1), preferred_element_type=jnp.float32
    ).astype(jnp.bfloat16)
    return [
        right_side(moved[:, n * width : (n + 1) * width], turned_cols[n]).astype(jnp.bfloat16)
        for n in range(len(blocks))
    ]


def kernel(
    span, feat, adj, cols, m1, m2, fin_a, fin_f,
    m1v, m2v, tab, raw_v, adj_v, feat_v, send_a, send_f, lev_a, lev_f,
    loc_sem, got_sem, sr_sem, send_sem, xr_sem,
):
    tiles, slots, width = adj.shape[0], adj.shape[1], adj.shape[2]
    quarter = tiles // 4
    groups = slots // GROUP
    blk, sub = lax.axis_index("blk"), lax.axis_index("sub")
    b, s = lax.rem(blk, 2), lax.rem(sub, 2)
    core = {"blk": blk + 1 - 2 * b}
    near = {"sub": sub + 1 - 2 * s}
    across = {"blk": blk + 1 - 2 * b, "sub": sub + 1 - 2 * s}
    subs = span // tiles
    first_pair = (blk // 2 * subs + sub) * tiles
    first_group = (blk // 2 * (subs // 2) + sub // 2) * tiles
    pairs, pairs2 = m1.shape[0], m2.shape[0]

    def side(j):
        return (1 - s) * (1 - j) + s * j

    def own_copy(j, i, part, n):
        return pltpu.make_async_copy(
            adj.at[4 * i + 2 * b + side(j), part], adj_v.at[b, j, i, part], got_sem.at[n]
        )

    def core_copy(j, i, part, n):
        return pltpu.make_async_remote_copy(
            src_ref=adj.at[4 * i + 2 * (1 - b) + side(j), part],
            dst_ref=adj_v.at[b, j, i, part],
            send_sem=send_sem, recv_sem=got_sem.at[n],
            device_id=core, device_id_type=MESH,
        )

    def sub_copy(i, k, n):
        return pltpu.make_async_remote_copy(
            src_ref=send_a.at[i * slots + k], dst_ref=lev_a.at[s, i, k],
            send_sem=send_sem, recv_sem=sr_sem.at[n],
            device_id=near, device_id_type=MESH,
        )

    def small(src, dst, n, device):
        return pltpu.make_async_remote_copy(
            src_ref=src, dst_ref=dst, send_sem=send_sem, recv_sem=xr_sem.at[n],
            device_id=device, device_id_type=MESH,
        )

    def all_of(ref, sem):
        pltpu.make_async_copy(ref, ref, sem).wait()

    barrier = pltpu.get_barrier_semaphore()
    pl.semaphore_signal(barrier, inc=1, device_id=core, device_id_type=MESH)
    pl.semaphore_signal(barrier, inc=1, device_id=near, device_id_type=MESH)
    pl.semaphore_signal(barrier, inc=1, device_id=across, device_id_type=MESH)

    local = [
        pltpu.make_async_copy(m1, m1v.at[pl.ds(0, pairs)], loc_sem.at[0]),
        pltpu.make_async_copy(cols, tab.at[b], loc_sem.at[1]),
        pltpu.make_async_copy(m2, m2v.at[pl.ds(0, pairs2)], loc_sem.at[2]),
        pltpu.make_async_copy(feat, feat_v.at[b], xr_sem.at[2]),
    ]
    whole = pl.ds(0, slots)
    edges = (RAW, GROUP, 2 * GROUP, slots)
    first = [pl.ds(low, high - low) for low, high in zip(edges, edges[1:])]
    heads = len(first) - 1
    last = quarter - 1
    plain = lax.broadcasted_iota(jnp.int32, (8, width), 1)
    m1v[pl.ds(pairs, 8), :] = plain
    m2v[pl.ds(pairs2, 8), :] = plain

    def load_first():
        local[1].start()
        for q in range(heads + 1):
            own_copy(0, 0, first[q], q).start()
        local[0].start()

    @pl.when(b == 1)
    def _():
        load_first()
        local[3].start()
        own_copy(0, 1, whole, 3).start()

    pl.semaphore_wait(barrier, 3)
    early = pl.ds(0, RAW)
    cols_core = small(cols, tab.at[b], 0, core)
    cols_near = small(cols, tab.at[2], 1, near)
    cols_across = small(cols, tab.at[3], 3, across)
    feat_core = small(feat, feat_v.at[b], 2, core)
    raw_near = small(adj.at[2 * b + side(0), early], raw_v.at[b], 4, near)
    raw_across = small(adj.at[2 * (1 - b) + side(0), early], raw_v.at[b], 4, across)
    core_copy(0, 0, first[0], 0).start()
    cols_core.start()
    raw_near.start()
    raw_across.start()
    for q in range(1, heads + 1):
        core_copy(0, 0, first[q], q).start()
    pl.when(b == 0)(load_first)
    feat_core.start()
    cols_near.start()
    cols_across.start()
    pl.when(b == 0)(local[3].start)

    core_copy(0, 1, whole, 3).start()
    pl.when(b == 0)(own_copy(0, 1, whole, 3).start)


    local[0].wait()
    local[1].wait()
    cols_core.wait_recv()

    def columns(table, maps, plain_row, tile, k, bit, row):
        hots = []
        for part in range(2):
            upper = lax.rem(tab[table[part], k, tile] // bit, 2)
            here = maps[pl.ds(upper * row + (1 - upper) * plain_row, 1), :]
            hots.append(turned(here, width))
        return jnp.concatenate(hots, axis=1)

    def first_rows(tile):
        return turned(m1v[pl.ds(first_pair + tile, 1), :], width)

    def first_level(j, i, store, parts, start=0):
        tile = 4 * i + 2 * b + side(j)
        rows = first_rows(tile)
        for q in range(groups):
            for part, n in parts.get(q, ()):
                all_of(adj_v.at[:, j, i, part], got_sem.at[n])
            ks = range(max(start, q * GROUP), (q + 1) * GROUP)
            if not ks:
                continue
            hots = []
            for k in ks:
                c = tab[b, k, tile]
                p = c // (2 * span) * span + lax.rem(c, span)
                hots.append(columns((0, 1), m1v, pairs, tile, k, span, p))
            done = merged(
                [adj_v[0, j, i, k] for k in ks], [adj_v[1, j, i, k] for k in ks], rows, hots
            )
            store(i, ks, done)
        return tile, rows

    def feature_level(j, i, tile, rows, dst):
        at = pl.ds(pl.multiple_of(tile * width, width), width)
        total = feat_v[0, :, at].astype(jnp.float32) + right_side(feat_v[1, :, at], rows)
        dst[:, pl.ds(pl.multiple_of(i * width, width), width)] = total.astype(jnp.bfloat16)

    def arrival(i, k):
        return last + LAST[k] if isinstance(i, int) and i == last else i

    def own_second(j, ks, done):
        tile = 4 * last + 2 * b + side(j)
        high = s * (first_group + tile) + (1 - s) * pairs2
        rows = turned(m2v[pl.ds(high, 1), :], width)
        hots = []
        for k in ks:
            c = tab[b, k, tile]
            p = c // (2 * span) * span + lax.rem(c, span)
            g = p // (2 * tiles) * tiles + lax.rem(p, tiles)
            upper = lax.rem(c // tiles, 2)
            hots.append(turned(m2v[pl.ds(upper * g + (1 - upper) * pairs2, 1), :], width))
        return carried(done, rows, hots)

    def store_send(i, ks, done):
        if i == last:
            done = own_second(0, ks, done)
        for k, block in zip(ks, done):
            send_a[i * slots + k] = block

        @pl.when(b == 1)
        def _():
            for k in ks:
                sub_copy(i, k, arrival(i, k)).start()

    def send_tile(i, begin):
        @pl.when(b == 0)
        def _():
            for k in range(begin, slots):
                sub_copy(i, k, arrival(i, k)).start()


    def store_keep(i, ks, done):
        if isinstance(i, int):
            done = own_second(1, ks, done)
        for k, block in zip(ks, done):
            lev_a[s, i, k] = block

    first_level(0, 0, store_send, {q: [(first[q], q)] for q in range(heads + 1)}, RAW)

    @pl.loop(2, quarter)
    def _(i):
        core_copy(0, i, whole, 4).start()
        own_copy(0, i, whole, 4).start()

    @pl.loop(0, quarter)
    def _(i):
        core_copy(1, i, whole, 5).start()
        own_copy(1, i, whole, 5).start()

    local[2].start()
    all_of(feat_v, xr_sem.at[2])
    for i in range(quarter):
        tile = 4 * i + 2 * b + side(0)
        feature_level(0, i, tile, first_rows(tile), send_f)
    feat_near = small(send_f, lev_f.at[s], 5, near)
    feat_near.start()

    for i in range(1, quarter):
        if i == last:
            local[2].wait()
        if i == 2:
            all_of(adj_v.at[:, 0, pl.ds(2, quarter - 2)], got_sem.at[4])
        first_level(0, i, store_send, {0: [(whole, 3)]} if i == 1 else {})
        if i >= LAG:
            send_tile(i - LAG, RAW if i == LAG else 0)
    for i in range(quarter - LAG, quarter):
        send_tile(i, RAW if i == 0 else 0)

    def keep(i):
        tile, rows = first_level(1, i, store_keep, {})
        feature_level(1, i, tile, rows, lev_f.at[s])

    all_of(adj_v.at[:, 1], got_sem.at[5])
    pl.loop(0, last)(keep)
    keep(last)

    cols_near.wait_recv()
    cols_across.wait_recv()
    all_of(raw_v, xr_sem.at[4])
    there = 2 * b + s
    near_pair = (blk // 2 * subs + sub + 1 - 2 * s) * tiles
    near_rows = turned(m1v[pl.ds(near_pair + there, 1), :], width)
    hots = []
    for k in range(RAW):
        c = tab[2, k, there]
        p = c // (2 * span) * span + lax.rem(c, span)
        mine = lax.rem(c // span, 2)
        other = lax.rem(tab[3, k, there] // span, 2)
        parts = []
        for upper in (b * other + (1 - b) * mine, b * mine + (1 - b) * other):
            row = upper * p + (1 - upper) * pairs
            parts.append(turned(m1v[pl.ds(row, 1), :], width))
        hots.append(jnp.concatenate(parts, axis=1))
    done = merged(
        [raw_v[0, k] for k in range(RAW)], [raw_v[1, k] for k in range(RAW)], near_rows, hots
    )
    for k in range(RAW):
        lev_a[1 - s, 0, k] = done[k]

    def second_rows(tile):
        return turned(m2v[pl.ds(first_group + tile, 1), :], width)

    def second_level(i, begin):
        tile = 4 * i + 2 * b + s
        rows = second_rows(tile)
        for k in range(slots):
            c = tab[b, k, tile]
            p = c // (2 * span) * span + lax.rem(c, span)
            g = p // (2 * tiles) * tiles + lax.rem(p, tiles)
            hots = columns((b * (1 - s) + 2 * s, b * s + 2 * (1 - s)), m2v, pairs2, tile, k, tiles, g)
            if k == begin:
                all_of(lev_a.at[1 - s, i, pl.ds(k, slots - k)], sr_sem.at[i])
            fin_a[i, k] = merged([lev_a[0, i, k]], [lev_a[1, i, k]], rows, [hots])[0]

    second_level(0, RAW)

    @pl.loop(1, last)
    def _(i):
        second_level(i, 0)

    feat_near.wait_recv()
    for i in range(quarter):
        at = pl.ds(i * width, width)
        rows = second_rows(4 * i + 2 * b + s)
        total = lev_f[0, :, at].astype(jnp.float32) + right_side(lev_f[1, :, at], rows)
        fin_f[:, at] = total.astype(jnp.bfloat16)

    for n in range(max(LAST) + 1):
        part = pl.ds(LAST.index(n), LAST.count(n))
        all_of(lev_a.at[1 - s, last, part], sr_sem.at[last + n])
        total = lev_a[0, last, part].astype(jnp.float32) + lev_a[1, last, part].astype(jnp.float32)
        fin_a[last, part] = total.astype(jnp.bfloat16)

    all_of(adj_v.at[0, 0, 0, pl.ds(RAW, slots - RAW)], send_sem)
    all_of(adj_v.at[0, 0, pl.ds(1, last)], send_sem)
    all_of(adj_v.at[0, 1], send_sem)
    all_of(send_a.at[pl.ds(RAW, quarter * slots - RAW)], send_sem)
    for copy in (cols_core, cols_near, cols_across, feat_core, feat_near, raw_near, raw_across):
        copy.wait_send()


def put(tiles, feats, out_a, out_f, sem):
    copies = [
        pltpu.make_async_copy(tiles, out_a, sem.at[0]),
        pltpu.make_async_copy(feats, out_f, sem.at[1]),
    ]
    for copy in copies:
        copy.start()
    for copy in copies:
        copy.wait()


def per_device(features, adjacency, col_tiles, match_one, match_two):
    tiles, slots, width = adjacency.shape[:3]
    feats = features.shape[0]
    quarter, groups = tiles // 4, slots // GROUP
    span = lax.axis_size("sub") * tiles
    half = jnp.bfloat16

    def outside(part):
        return pltpu.with_memory_space_constraint(part, pltpu.HBM)

    dma = pltpu.SemaphoreType.DMA
    anywhere = pl.BlockSpec(memory_space=pltpu.HBM)
    inside = pl.BlockSpec(memory_space=pltpu.VMEM)
    tile_out = ((quarter, slots, width, width), half)
    feat_out = ((feats, quarter * width), half)
    done = pl.pallas_call(
        functools.partial(kernel, span),
        out_shape=(pltpu.VMEM(*tile_out), pltpu.VMEM(*feat_out)),
        in_specs=[anywhere] * 5,
        out_specs=(inside, inside),
        scratch_shapes=[
            pltpu.VMEM((match_one.shape[0] + 8, width), jnp.int32),
            pltpu.VMEM((match_two.shape[0] + 8, width), jnp.int32),
            pltpu.SMEM((4, slots, tiles), jnp.int32),
            pltpu.VMEM((2, RAW, width, width), half),
            pltpu.VMEM((2, 2, quarter, slots, width, width), half),
            pltpu.VMEM((2,) + features.shape, half),
            pltpu.VMEM((quarter * slots, width, width), half),
            pltpu.VMEM((feats, quarter * width), half),
            pltpu.VMEM((2, quarter, slots, width, width), half),
            pltpu.VMEM((2, feats, quarter * width), half),
            dma((3,)),
            dma((6,)),
            dma((quarter + max(LAST),)),
            dma,
            dma((6,)),
        ],
        compiler_params=pltpu.CompilerParams(
            collective_id=0, has_side_effects=True, vmem_limit_bytes=VMEM_BYTES
        ),
        name="coarsen",
    )(*(outside(part) for part in (features, adjacency, col_tiles.T, match_one, match_two)))
    return pl.pallas_call(
        put,
        out_shape=(jax.ShapeDtypeStruct(*tile_out), jax.ShapeDtypeStruct(*feat_out)),
        in_specs=[inside] * 2,
        out_specs=(anywhere, anywhere),
        scratch_shapes=[dma((2,))],
        name="put",
    )(*(pltpu.with_memory_space_constraint(part, pltpu.VMEM) for part in done))


def solution(mesh):
    placed = (
        P(None, ("blk", "sub")),
        P(("blk", "sub"), None, None, None),
        P(("blk", "sub"), None),
        P(),
        P(),
    )
    return jax.shard_map(
        per_device,
        mesh=mesh,
        in_specs=placed,
        out_specs=(P(("blk", "sub"), None, None, None), P(None, ("blk", "sub"))),
        check_vma=False,
    )
```
